32 devices in a mesh: groups: 2 (over y), ep: 4 (over z), side: 2 (over core), head: 2 (over x).
Axes of the slice: x: 2, y: 2, z: 4, core: 2. Of those that a mesh axis runs over, the one named last changes fastest.
Arguments:
- hidden: bfloat16 [64, 2048], P(('groups', 'ep')), parts along dimension 0, may hold values from -6 to 6
- query: bfloat16 [64, 4, 1024], P(('groups', 'ep'), 'head', 'side'), parts along dimension 0, may hold values from -6 to 6
- new_key: bfloat16 [64, 512], P(('groups', 'ep'), 'head'), parts along dimension 0, may hold values from -220 to 220
- new_value: bfloat16 [64, 512], P(('groups', 'ep'), 'head'), parts along dimension 0, may hold values from -6 to 6
- cache_keys: bfloat16 [64, 128, 512], P(('groups', 'ep'), None, 'head'), parts along dimension 0, may hold values from -220 to 220
- cache_values: bfloat16 [64, 128, 512], P(('groups', 'ep'), None, 'head'), parts along dimension 0, may hold values from -6 to 6
- lengths: int32 [64], P(('groups', 'ep')), parts along dimension 0, may hold values from 1 to 128, 1024 in all
- out_weight: bfloat16 [4, 1024, 2048], P('head', 'side'), may hold values from -0.14 to 0.14
- norm_gain: float32 [2048], replicated, may hold values from 0.5 to 1.5
- expert_ids: int32 [64, 8], P(('groups', 'ep')), parts along dimension 0, may hold values from 0 to 63, all different within a row; in each aligned block of 8 rows (0 to 7, 8 to 15, ...) at most 2 rows name the same one
- route_weights: float32 [64, 8], P(('groups', 'ep')), parts along dimension 0, may hold values from 0.25 to 1
- gate_weight: bfloat16 [64, 2048, 768], P(('ep', 'side'), None, 'head'), may hold values from -0.125 to 0.125
- up_weight: bfloat16 [64, 2048, 768], P(('ep', 'side'), None, 'head'), may hold values from -0.125 to 0.125
- down_weight: bfloat16 [64, 768, 2048], P(('ep', 'side'), 'head'), may hold values from -0.21875 to 0.21875
Outputs:
- after_attention: float32 [64, 2048], P(('groups', 'ep'), 'head'), parts along dimension 0
- expert_sum: bfloat16 [64, 2048], P(('groups', 'ep'), 'head'), parts along dimension 0
The draws below stay inside these ranges and needn't reach their ends.
There are 2 independent parts, one for each index of `groups`. The reference program is written for one: setup_inputs(seed, part) draws one part's arguments, and reference() takes and returns one part's arrays. A program takes and returns all parts, laid end to end along the dimension named above; an argument that names none is the same for every part. Nothing has to cross between parts.
Inputs may be any that keep to these rules, and one draw needn't show every extreme that they name: `expert_ids`: each row names 8 different experts; among the 8 aligned rows of one index of ep no expert is named more than 2 times, and some expert reaches 2.
All inputs are finite; a program needn't handle non-finite values. No bound on the sum of `lengths` on one device may be relied on, other than what follows from the above.
Results may differ from the reference program's by a relative error of at most 0.024.
Values may be sent and summed in bfloat16 or wider, within the bound.
No kernel may reach another device: no remote copies, remote signals or barrier semaphores. Data moves between devices by JAX's collectives and lax.ppermute only.
A program may use at most 128 MiB of HBM per device.

```python
import math
import jax
import jax.numpy as jnp
import numpy as np
from jax import lax

D = 2048
HD = 128
KVH = 4
QPK = 8
FF = 768
EXPERTS = 64
TOP = 8
CAP = 2
ROWS_EP = 8
CTX = 128
ROWS = 32


def query_base(key):
    drawn = jax.random.normal(jax.random.fold_in(key, 11), (ROWS, KVH, QPK * HD), jnp.float32)
    return jnp.clip(drawn, -6.0, 6.0).astype(jnp.bfloat16).astype(jnp.float32)


def draw_query(key, part):
    return query_base(key).astype(jnp.bfloat16)


def draw_new_key(key, part):
    sample = jnp.clip(jax.random.normal(jax.random.fold_in(key, 14), (ROWS, KVH, HD), jnp.float32), -6.0, 6.0)
    return sample.reshape(ROWS, KVH * HD).astype(jnp.bfloat16)


def draw_cache_keys(key, part):
    sample = jnp.clip(jax.random.normal(jax.random.fold_in(key, 15), (ROWS, CTX, KVH, HD), jnp.float32), -6.0, 6.0)
    return sample.reshape(ROWS, CTX, KVH * HD).astype(jnp.bfloat16)


def draw_hidden(key, part):
    base = jnp.clip(jax.random.normal(jax.random.fold_in(key, 21), (ROWS, D), jnp.float32), -6.0, 6.0)
    row_scale = jnp.exp(jax.random.uniform(jax.random.fold_in(key, 22), (ROWS, 1), jnp.float32, math.log(0.05), 0.0))
    return (base * row_scale).astype(jnp.bfloat16)


def draw_out_weight(key, part):
    shape_all = (KVH, QPK * HD, D)
    base = jnp.clip(jax.random.normal(jax.random.fold_in(key, 23), shape_all, jnp.float32), -4.0, 4.0)
    flip = jnp.where(jax.random.bernoulli(jax.random.fold_in(key, 24)), jnp.float32(1.0), jnp.float32(-1.0))
    ramp = (jnp.arange(D, dtype=jnp.float32) + 0.5) / D - 0.5
    level = jnp.exp(flip * ramp * math.log(10.0)) / math.sqrt(2.15)
    scaled = base * level[None, None, :] / math.sqrt(KVH * QPK * HD)
    return jnp.clip(scaled, -0.138, 0.138).astype(jnp.bfloat16)


def steps_of(rng, extent, cuts, least, high):
    level = 1.0
    for dim, shards_of in cuts:
        heights = jax.random.uniform(jax.random.fold_in(jax.random.fold_in(rng, 6), dim), (shards_of,), jnp.float32, least / len(cuts), high / len(cuts))
        level = level * jnp.repeat(jnp.exp(heights), extent[dim] // shards_of).reshape((-1,) + (1,) * (len(extent) - 1 - dim))
    return level


def length_profile(number_of, total, reach, slope):
    weights = [(1 << 20) // math.isqrt(rank ** slope) + 1 for rank in range(2, number_of + 1)]
    rest, given = total - reach - (number_of - 1), [1] * (number_of - 1)
    while rest > 0:
        free = [i for i in range(number_of - 1) if given[i] < reach]
        whole, left = sum([weights[i] for i in free]), rest
        for i in free:
            more = min(reach - given[i], max(1, left * weights[i] // whole), rest)
            given[i] = given[i] + more
            rest = rest - more
    return np.array([reach] + given)


def ragged_sizes(key, count, total, reach, skew):
    if count == 2:
        one = jax.random.randint(key, (), max(1, total - reach), min(reach, total - 1) + 1)
        return jnp.stack([one, total - one])
    tallies = jnp.asarray(length_profile(count, total, reach, skew), jnp.int32)
    pairs = (count - 1) // 2
    giver, receiver = tallies[1:1 + 2 * pairs:2], tallies[2:2 + 2 * pairs:2]
    slack = jnp.minimum(giver - 1, reach - receiver)
    shifted = jax.random.randint(jax.random.fold_in(key, 1), (pairs,), 0, 1 << 20) % (slack + 1)
    tallies = tallies.at[1:1 + 2 * pairs:2].set(giver - shifted).at[2:2 + 2 * pairs:2].set(receiver + shifted)
    return tallies[jax.random.permutation(jax.random.fold_in(key, 2), count)]


def deal_out(rng, own, number, rows, amount, top, most, slope):
    order = jax.random.permutation(rng, amount)
    packed, ordinary = load_shares(amount, rows * top, most, slope, True), load_shares(amount, rows * top, most, slope, False)
    places = jnp.arange(amount)

    def named(sizes, turn):
        used = int((sizes > 0).sum())
        fixed = max(1, used // 4)
        passed = fixed + (places - fixed + turn * (used - fixed)) % max(1, amount - fixed)
        return jnp.zeros((amount,), jnp.int32).at[order[jnp.where(places < fixed, places, passed)]].set(jnp.asarray(sizes, jnp.int32))

    sizes = jnp.where(number % 4 == 0, named(packed, number // 4), named(ordinary, number - number // 4 - 1))
    mixed = jax.random.permutation(jax.random.fold_in(own, 3), amount)
    donor, sink = mixed[0:amount // 2 * 2:2], mixed[1:amount // 2 * 2:2]
    margin = jnp.minimum(sizes[donor] - 1, most - sizes[sink]) // 2
    margin = jnp.where((donor == order[0]) | (sink == order[0]) | (sizes[sink] == 0), 0, jnp.maximum(margin, 0))
    passed = jax.random.randint(jax.random.fold_in(own, 4), (amount // 2,), 0, 1 << 20) % (margin + 1)
    sizes = sizes.at[donor].add(-passed).at[sink].add(passed)
    items = jnp.searchsorted(jnp.cumsum(sizes), jnp.arange(rows * top), side="right").astype(jnp.int32)
    table = items.reshape(top, rows).T
    table = table[jax.random.permutation(jax.random.fold_in(own, 1), rows)]
    turn = jax.random.randint(jax.random.fold_in(own, 2), (rows, 1), 0, top)
    return jnp.take_along_axis(table, (jnp.arange(top)[None, :] + turn) % top, axis=1)


def load_shares(number_of, total, limit, skew, full):
    loads = [(1 << 20) // math.isqrt(rank ** skew) + 1 for rank in range(1, number_of + 1)]
    largest = limit if full else min(limit, max(-(-total // number_of), total * loads[0] // sum(loads)))
    least = 1 if total - largest >= number_of - 1 else 0
    counts, spare = [largest] + [least] * (number_of - 1), total - largest - least * (number_of - 1)
    while spare > 0:
        movable = [i for i in range(1, number_of) if counts[i] < largest] or [i for i in range(1, number_of) if counts[i] < limit]
        whole, left = sum([loads[i] for i in movable]), spare
        for i in movable:
            extra = min(limit - counts[i], max(1, left * loads[i] // whole), spare)
            counts[i] = counts[i] + extra
            spare = spare - extra
    return np.array(counts)


def bell_draw(rng, extent, width, reach, cuts=(), held_as=jnp.bfloat16):
    factor_of = steps_of(rng, extent, cuts, -0.22, 0.18) if cuts else 1.0
    entries = jax.random.normal(rng, extent, jnp.float32) * width * factor_of
    return jnp.minimum(jnp.maximum(entries, -reach), reach).astype(held_as)


def setup_inputs(seed: int = 0, part: int = 0) -> dict:
    streams_of = jax.random.split(jax.random.key(seed), 15)
    part_splits = jax.random.split(jax.random.fold_in(streams_of[14], part), 15)
    hidden = draw_hidden(jax.random.fold_in(jax.random.fold_in(streams_of[14], part), 71), part)
    query = draw_query(jax.random.fold_in(jax.random.fold_in(streams_of[14], part), 71), part)
    new_key = draw_new_key(jax.random.fold_in(jax.random.fold_in(streams_of[14], part), 71), part)
    new_value = bell_draw(part_splits[3], (ROWS, KVH * HD), 1.0, 6.0, ((0, 4), (1, 2)))
    cache_keys = draw_cache_keys(jax.random.fold_in(jax.random.fold_in(streams_of[14], part), 71), part)
    cache_values = bell_draw(part_splits[5], (ROWS, CTX, KVH * HD), 1.0, 6.0, ((0, 4), (2, 2)))
    lengths = ragged_sizes(part_splits[6], ROWS, ROWS * (CTX // 4), CTX, 2).astype(jnp.int32)
    out_weight = draw_out_weight(jax.random.fold_in(streams_of[14], 71), part)
    norm_gain = jnp.clip(1.0 + 0.1 * jax.random.normal(streams_of[8], (D,), jnp.float32), 0.5, 1.5)
    expert_ids_keys = jax.random.split(jax.random.fold_in(part_splits[9], 1), ROWS // ROWS_EP)
    expert_ids_turns = jax.random.permutation(jax.random.fold_in(part_splits[9], 3), ROWS // ROWS_EP)
    expert_ids = jax.vmap(lambda own, number: deal_out(jax.random.fold_in(part_splits[9], 2), own, number, ROWS_EP, EXPERTS, TOP, CAP, 2))(expert_ids_keys, expert_ids_turns).reshape((ROWS, TOP))
    route_weights = jnp.clip(jnp.exp(math.log(1.0) - 1.3862944 * jax.random.uniform(part_splits[10], (ROWS, TOP), jnp.float32) ** steps_of(part_splits[10], (ROWS, TOP), ((0, 4),), -0.2, 0.2)), 0.25, 1.0)
    gate_weight = bell_draw(streams_of[11], (EXPERTS, D, FF), D ** -0.5, 0.125, ((0, 8), (2, 2)))
    up_weight = bell_draw(streams_of[12], (EXPERTS, D, FF), D ** -0.5, 0.125, ((0, 8), (2, 2)))
    down_weight = bell_draw(streams_of[13], (EXPERTS, FF, D), FF ** -0.5, 0.21875, ((0, 8), (1, 2)))
    return {"hidden": hidden, "query": query, "new_key": new_key, "new_value": new_value, "cache_keys": cache_keys, "cache_values": cache_values, "lengths": lengths, "out_weight": out_weight, "norm_gain": norm_gain, "expert_ids": expert_ids, "route_weights": route_weights, "gate_weight": gate_weight, "up_weight": up_weight, "down_weight": down_weight}


def reference(hidden, query, new_key, new_value, cache_keys, cache_values, lengths, out_weight, norm_gain, expert_ids, route_weights, gate_weight, up_weight, down_weight):
    scale = 1.0 / math.sqrt(HD)
    queries = query.astype(jnp.float32).reshape(ROWS, KVH, QPK, HD)
    cached_keys = cache_keys.astype(jnp.float32).reshape(ROWS, CTX, KVH, HD)
    cached_values = cache_values.astype(jnp.float32).reshape(ROWS, CTX, KVH, HD)
    fresh_key = new_key.astype(jnp.float32).reshape(ROWS, KVH, HD)
    fresh_value = new_value.astype(jnp.float32).reshape(ROWS, KVH, HD)
    scores = jnp.einsum('rgnd,rcgd->rgnc', queries, cached_keys) * scale
    fresh = jnp.einsum('rgnd,rgd->rgn', queries, fresh_key) * scale
    usable = jnp.arange(CTX, dtype=jnp.int32)[None, :] < lengths[:, None]
    scores = jnp.where(usable[:, None, None, :], scores, jnp.float32(-1e+30))
    highest = jnp.maximum(lax.optimization_barrier(jnp.max(scores, -1)), fresh)
    weights = jnp.where(usable[:, None, None, :], jnp.exp(scores - highest[..., None]), jnp.float32(0.0))
    own_weight = jnp.exp(fresh - highest)
    denominator = lax.optimization_barrier(jnp.sum(weights, -1)) + own_weight
    weights_low = weights.astype(jnp.bfloat16).astype(jnp.float32)
    own_low = own_weight.astype(jnp.bfloat16).astype(jnp.float32)
    mixed = jnp.einsum('rgnc,rcgd->rgnd', weights_low, cached_values) + own_low[..., None] * fresh_value[:, :, None, :]
    attended = (mixed / denominator[..., None]).astype(jnp.bfloat16).reshape(ROWS, KVH * QPK * HD)
    projected = jnp.dot(attended, out_weight.reshape(KVH * QPK * HD, D), preferred_element_type=jnp.float32)
    stream = hidden.astype(jnp.float32) + projected
    normed = (stream * lax.rsqrt(lax.optimization_barrier(jnp.mean(stream * stream, -1, keepdims=True)) + 1e-06) * norm_gain).astype(jnp.bfloat16)
    share = route_weights / lax.optimization_barrier(jnp.sum(route_weights, 1, keepdims=True))
    matches = expert_ids[:, :, None] == jnp.arange(EXPERTS, dtype=jnp.int32)[None, None, :]
    coefficient = lax.optimization_barrier(jnp.sum(jnp.where(matches, share[:, :, None], jnp.float32(0.0)), 1))

    def expert_step(running, pieces):
        gate_part, up_part, down_part, column = pieces
        gate = jnp.dot(normed, gate_part, preferred_element_type=jnp.float32)
        upper = jnp.dot(normed, up_part, preferred_element_type=jnp.float32)
        inner = (jax.nn.silu(gate) * upper).astype(jnp.bfloat16)
        result = jnp.dot(inner, down_part, preferred_element_type=jnp.float32).astype(jnp.bfloat16)
        return (running + column[:, None] * result.astype(jnp.float32), None)
    start_sum = jnp.zeros((ROWS, D), jnp.float32)
    summed, _ = lax.scan(expert_step, start_sum, (gate_weight, up_weight, down_weight, coefficient.T))
    return (stream, summed.astype(jnp.bfloat16))
```

```python
import math

import jax
import jax.numpy as jnp
from jax import lax
from jax.sharding import PartitionSpec as P

HD = 128
BF = jnp.bfloat16
F32 = jnp.float32


def partners(count):
    steps = []
    k = 1
    while k < count:
        steps.append(k)
        k *= 2
    return steps


def swap(x, axis, k):
    count = lax.axis_size(axis)
    return lax.ppermute(x, axis, [(i, i ^ k) for i in range(count)])


def sum_over(x, axis):
    for k in partners(lax.axis_size(axis)):
        low = x.astype(BF)
        x = low.astype(F32) + swap(low, axis, k).astype(F32)
    return x


def on_device(
    hidden,
    query,
    new_key,
    new_value,
    cache_keys,
    cache_values,
    lengths,
    out_weight,
    norm_gain,
    expert_ids,
    route_weights,
    gate_weight,
    up_weight,
    down_weight,
):
    ep_count = lax.axis_size("ep")
    side_count = lax.axis_size("side")
    head_count = lax.axis_size("head")
    rows_here = hidden.shape[0]
    context = cache_keys.shape[1]
    kv_local = new_key.shape[1] // HD
    scale = 1.0 / math.sqrt(HD)
    queries = query.reshape(rows_here, kv_local, -1, HD)
    cached_keys = cache_keys.reshape(rows_here, context, kv_local, HD)
    cached_values = cache_values.reshape(rows_here, context, kv_local, HD)
    fresh_key = new_key.reshape(rows_here, kv_local, HD)
    fresh_value = new_value.reshape(rows_here, kv_local, HD)
    scores = (
        jnp.einsum("rgnd,rcgd->rgnc", queries, cached_keys, preferred_element_type=F32) * scale
    )
    fresh = jnp.einsum("rgnd,rgd->rgn", queries, fresh_key, preferred_element_type=F32) * scale
    usable = jnp.arange(context, dtype=jnp.int32)[None, :] < lengths[:, None]
    scores = jnp.where(usable[:, None, None, :], scores, F32(-1e30))
    highest = jnp.maximum(jnp.max(scores, -1), fresh)
    weights = jnp.where(usable[:, None, None, :], jnp.exp(scores - highest[..., None]), F32(0.0))
    own_weight = jnp.exp(fresh - highest)
    denominator = jnp.sum(weights, -1) + own_weight
    mixed = jnp.einsum(
        "rgnc,rcgd->rgnd", weights.astype(BF), cached_values, preferred_element_type=F32
    )
    own_low = own_weight.astype(BF).astype(F32)
    mixed = mixed + own_low[..., None] * fresh_value.astype(F32)[:, :, None, :]
    attended = (mixed / denominator[..., None]).astype(BF).reshape(rows_here, -1)
    partial_value = jnp.dot(
        attended, out_weight.reshape(-1, out_weight.shape[2]), preferred_element_type=F32
    )
    projected = sum_over(sum_over(partial_value, "side"), "head")
    stream = hidden.astype(F32) + projected
    width = stream.shape[1] // head_count
    head_index = lax.axis_index("head")
    after_attention = lax.dynamic_slice_in_dim(stream, head_index * width, width, 1)
    normed = (
        stream * lax.rsqrt(jnp.mean(stream * stream, -1, keepdims=True) + 1e-06) * norm_gain
    ).astype(BF)

    local_count = gate_weight.shape[0]
    experts = local_count * ep_count * side_count
    share = route_weights / jnp.sum(route_weights, 1, keepdims=True)
    named = expert_ids[:, :, None] == jnp.arange(experts, dtype=jnp.int32)[None, None, :]
    coefficient = jnp.sum(jnp.where(named, share[:, :, None], F32(0.0)), 1)
    high = coefficient.astype(BF)
    low = (coefficient - high.astype(F32)).astype(BF)
    packed = jnp.concatenate([normed, high, low], 1)
    for k in partners(ep_count):
        packed = jnp.concatenate([packed, swap(packed, "ep", k)], 0)
    depth = normed.shape[1]
    gathered = packed[:, :depth]
    coefficient = packed[:, depth : depth + experts].astype(F32) + packed[:, depth + experts :].astype(F32)
    first = (lax.axis_index("ep") * side_count + lax.axis_index("side")) * local_count
    coefficient = lax.dynamic_slice_in_dim(coefficient, first, local_count, 1)
    gate = jnp.einsum("nd,ldf->lnf", gathered, gate_weight, preferred_element_type=F32)
    upper = jnp.einsum("nd,ldf->lnf", gathered, up_weight, preferred_element_type=F32)
    inner = (jax.nn.silu(gate) * upper * coefficient.T[:, :, None]).astype(BF)
    result = jnp.einsum("lnf,lfd->nd", inner, down_weight, preferred_element_type=F32)
    parts = head_count
    for k in reversed(partners(head_count)):
        half = result.shape[1] // 2
        upper_half = (head_index & k) != 0
        mine = jnp.where(upper_half, result[:, half:], result[:, :half])
        other = jnp.where(upper_half, result[:, :half], result[:, half:])
        result = mine.astype(F32) + swap(other.astype(BF), "head", k).astype(F32)
    for k in reversed(partners(ep_count)):
        half = result.shape[0] // 2
        result = result[:half] + swap(result[half:].astype(BF), "ep", k).astype(F32)
    expert_sum = sum_over(result, "side").astype(BF)
    return (after_attention, expert_sum)


def solution(mesh):
    placed = (
        P(("groups", "ep"), None),
        P(("groups", "ep"), "head", "side"),
        P(("groups", "ep"), "head"),
        P(("groups", "ep"), "head"),
        P(("groups", "ep"), None, "head"),
        P(("groups", "ep"), None, "head"),
        P(("groups", "ep")),
        P("head", "side", None),
        P(),
        P(("groups", "ep"), None),
        P(("groups", "ep"), None),
        P(("ep", "side"), None, "head"),
        P(("ep", "side"), None, "head"),
        P(("ep", "side"), "head", None),
    )
    return jax.shard_map(
        on_device,
        mesh=mesh,
        in_specs=placed,
        out_specs=(P(("groups", "ep"), "head"), P(("groups", "ep"), "head")),
        check_vma=False,
    )
```

```python
import functools
import math

import jax
import jax.numpy as jnp
from jax import lax
from jax.experimental import pallas as pl
from jax.experimental.pallas import tpu as pltpu
from jax.sharding import PartitionSpec as P

HD = 128
BF = jnp.bfloat16
F32 = jnp.float32
VMEM = pl.BlockSpec(memory_space=pltpu.VMEM)
HBM = pl.BlockSpec(memory_space=pltpu.HBM)


def in_vmem(x):
    return pltpu.with_memory_space_constraint(x, pltpu.VMEM)


def in_hbm(x):
    return pltpu.with_memory_space_constraint(x, pltpu.HBM)


def partners(count):
    steps = []
    k = 1
    while k < count:
        steps.append(k)
        k *= 2
    return steps


def swap(x, axis, k):
    count = lax.axis_size(axis)
    return lax.ppermute(x, axis, [(i, i ^ k) for i in range(count)])


def sum_over(low, axis):
    total = low.astype(F32)
    for k in partners(lax.axis_size(axis)):
        low = total.astype(BF)
        total = low.astype(F32) + swap(low, axis, k).astype(F32)
    return total


def attend_kernel(
    lengths_hbm,
    query_hbm,
    new_key_hbm,
    new_value_hbm,
    cache_keys_hbm,
    cache_values_hbm,
    expert_ids_hbm,
    route_weights_hbm,
    hidden_hbm,
    norm_gain_hbm,
    out_weight_hbm,
    attended_out,
    coefficient_out,
    hidden_out,
    norm_gain_out,
    out_weight_out,
    lengths,
    query,
    new_key,
    new_value,
    cache_keys,
    cache_values,
    expert_ids,
    route_weights,
    arrivals,
):
    moves = [
        (lengths_hbm, lengths),
        (query_hbm, query),
        (cache_keys_hbm, cache_keys),
        (new_key_hbm, new_key),
        (new_value_hbm, new_value),
        (cache_values_hbm, cache_values),
        (expert_ids_hbm, expert_ids),
        (route_weights_hbm, route_weights),
        (hidden_hbm, hidden_out),
        (norm_gain_hbm, norm_gain_out),
        (out_weight_hbm, out_weight_out),
    ]
    copies = [
        pltpu.make_async_copy(source, target, arrivals.at[i])
        for i, (source, target) in enumerate(moves)
    ]
    for copy in copies:
        copy.start()
    rows, kv_local, width = query.shape
    context = cache_keys.shape[1]
    heads = width // HD
    total = rows * context
    scale = 1.0 / math.sqrt(HD)
    pairs = [(g, n) for g in range(kv_local) for n in range(heads)]
    for copy in copies[:4]:
        copy.wait()
    zero = jnp.zeros((rows, HD), BF)
    queries = [query[:, g, n * HD : (n + 1) * HD] for g, n in pairs]
    placed = [
        jnp.concatenate([q if g == other else zero for other in range(kv_local)], 1)
        for (g, n), q in zip(pairs, queries)
    ]
    stacked = jnp.concatenate(placed, 0)
    keys = cache_keys[...].reshape(total, kv_local * HD)
    contract = (((1,), (1,)), ((), ()))
    scores = lax.dot_general(stacked, keys, contract, preferred_element_type=F32) * scale
    scores = scores.reshape(len(pairs), rows, total)
    row = lax.broadcasted_iota(jnp.int32, (rows, total), 0)
    column = lax.broadcasted_iota(jnp.int32, (rows, total), 1)
    start = row * context
    end = start
    for r in range(rows):
        end = jnp.where(row == r, r * context + lengths[r], end)
    usable = (column >= start) & (column < end)
    scores = jnp.where(usable[None], scores, F32(-1e30))
    fresh = jnp.stack(
        [
            jnp.sum(
                q.astype(F32) * new_key[:, g * HD : (g + 1) * HD].astype(F32), 1, keepdims=True
            )
            for (g, n), q in zip(pairs, queries)
        ],
        0,
    ) * scale
    highest = jnp.maximum(jnp.max(scores, -1, keepdims=True), fresh)
    weights = jnp.exp(scores - highest)
    own = jnp.exp(fresh - highest)
    denominator = jnp.sum(weights, -1, keepdims=True) + own
    low = weights.astype(BF).reshape(len(pairs) * rows, total)
    for copy in copies[4:8]:
        copy.wait()
    values = cache_values[...].reshape(total, kv_local * HD)
    mixed = jnp.dot(low, values, preferred_element_type=F32)
    mixed = mixed.reshape(len(pairs), rows, kv_local * HD)
    own_low = own.astype(BF).astype(F32)
    for i, (g, n) in enumerate(pairs):
        block = slice(g * HD, (g + 1) * HD)
        value = mixed[i][:, block] + own_low[i] * new_value[:, block].astype(F32)
        attended_out[:, i * HD : (i + 1) * HD] = (value / denominator[i]).astype(BF)
    experts = coefficient_out.shape[1] // 2
    weight = route_weights[...]
    share = weight / jnp.sum(weight, 1, keepdims=True)
    lane = lax.broadcasted_iota(jnp.int32, (rows, experts), 1)
    coefficient = jnp.zeros((rows, experts), F32)
    for k in range(weight.shape[1]):
        coefficient += jnp.where(lane == expert_ids[:, k : k + 1], share[:, k : k + 1], F32(0.0))
    high = coefficient.astype(BF)
    rest = (coefficient - high.astype(F32)).astype(BF)
    coefficient_out[...] = jnp.concatenate([high, rest], 1)
    for copy in copies[8:]:
        copy.wait()


def project_kernel(attended, out_weight, hidden, partial_out):
    depth = out_weight.shape[2]
    projected = jnp.dot(
        attended[...],
        out_weight[...].reshape(attended.shape[1], depth),
        preferred_element_type=F32,
    )
    first = (lax.axis_index("side") == 0) & (lax.axis_index("head") == 0)
    base = jnp.where(first, hidden[...].astype(F32), F32(0.0))
    partial_out[...] = (projected + base).astype(BF)


def expert_kernel(
    gathered, norm_gain, gate_weight, up_weight, down_weight, out, inner, width
):
    count, depth, hidden_units = gate_weight.shape
    experts = (gathered.shape[1] - depth) // 2
    rows = gathered.shape[0]
    stream = gathered[:, :depth].astype(F32)
    norm = lax.rsqrt(jnp.mean(stream * stream, -1, keepdims=True) + 1e-06)
    normed = (stream * norm * norm_gain[...]).astype(BF)
    coefficient = gathered[:, depth : depth + experts].astype(F32) + gathered[
        :, depth + experts :
    ].astype(F32)
    lane = lax.broadcasted_iota(jnp.int32, (rows, experts), 1)
    me = lax.axis_index("ep")
    first = (me * lax.axis_size("side") + lax.axis_index("side")) * count
    for e in range(count):
        gate = jnp.dot(normed, gate_weight[e], preferred_element_type=F32)
        upper = jnp.dot(normed, up_weight[e], preferred_element_type=F32)
        share = jnp.sum(jnp.where(lane == first + e, coefficient, F32(0.0)), 1, keepdims=True)
        value = gate / (1.0 + jnp.exp(-gate)) * upper * share
        inner[:, e * hidden_units : (e + 1) * hidden_units] = value.astype(BF)
    result = jnp.dot(
        inner[...],
        down_weight[...].reshape(count * hidden_units, depth),
        preferred_element_type=F32,
    ).astype(BF)
    blocks, block_rows, _ = out.shape
    heads = depth // width
    for j in range(blocks // heads):
        target = me ^ j
        for h in range(heads):
            out[target * heads + h] = result[
                j * block_rows : (j + 1) * block_rows, h * width : (h + 1) * width
            ]


def on_device(
    hidden,
    query,
    new_key,
    new_value,
    cache_keys,
    cache_values,
    lengths,
    out_weight,
    norm_gain,
    expert_ids,
    route_weights,
    gate_weight,
    up_weight,
    down_weight,
):
    ep_count = lax.axis_size("ep")
    side_count = lax.axis_size("side")
    head_count = lax.axis_size("head")
    head_index = lax.axis_index("head")
    rows, depth = hidden.shape
    local_count, _, hidden_units = gate_weight.shape
    experts = local_count * ep_count * side_count
    width = depth // head_count
    top = expert_ids.shape[1]
    gain = norm_gain.reshape(1, depth)
    attended, coefficient, hidden_near, gain_near, out_weight_near = pl.pallas_call(
        attend_kernel,
        out_shape=(
            pltpu.VMEM((rows, out_weight.shape[0] * out_weight.shape[1]), BF),
            pltpu.VMEM((rows, 2 * experts), BF),
            pltpu.VMEM(hidden.shape, BF),
            pltpu.VMEM(gain.shape, F32),
            pltpu.VMEM(out_weight.shape, BF),
        ),
        in_specs=[HBM] * 11,
        out_specs=(VMEM,) * 5,
        scratch_shapes=[
            pltpu.SMEM(lengths.shape, jnp.int32),
            pltpu.VMEM(query.shape, BF),
            pltpu.VMEM(new_key.shape, BF),
            pltpu.VMEM(new_value.shape, BF),
            pltpu.VMEM(cache_keys.shape, BF),
            pltpu.VMEM(cache_values.shape, BF),
            pltpu.VMEM((rows, top), jnp.int32),
            pltpu.VMEM((rows, top), F32),
            pltpu.SemaphoreType.DMA((11,)),
        ],
        compiler_params=pltpu.CompilerParams(vmem_limit_bytes=8 << 20),
        name="attend",
    )(
        in_hbm(lengths),
        in_hbm(query),
        in_hbm(new_key),
        in_hbm(new_value),
        in_hbm(cache_keys),
        in_hbm(cache_values),
        in_hbm(expert_ids),
        in_hbm(route_weights),
        in_hbm(hidden),
        in_hbm(gain),
        in_hbm(out_weight),
    )
    partial_value = pl.pallas_call(
        project_kernel,
        out_shape=pltpu.VMEM((rows, depth), BF),
        in_specs=[VMEM] * 3,
        out_specs=VMEM,
        compiler_params=pltpu.CompilerParams(vmem_limit_bytes=8 << 20),
        cost_estimate=pl.CostEstimate(
            flops=10**12, bytes_accessed=200 * 10**6, transcendentals=0
        ),
        name="project",
    )(in_vmem(attended), in_vmem(out_weight_near), in_vmem(hidden_near))
    stream = sum_over(sum_over(partial_value, "side").astype(BF), "head")
    after_attention = lax.dynamic_slice_in_dim(stream, head_index * width, width, 1)
    packed = jnp.concatenate([stream.astype(BF), coefficient], 1)
    if ep_count <= 4:
        gathered = jnp.concatenate(
            [packed] + [swap(packed, "ep", k) for k in range(1, ep_count)], 0
        )
    else:
        gathered = packed
        for k in partners(ep_count):
            gathered = jnp.concatenate([gathered, swap(gathered, "ep", k)], 0)
    weight_bytes = 2 * (gate_weight.size + up_weight.size + down_weight.size)
    result = pl.pallas_call(
        functools.partial(expert_kernel, width=width),
        out_shape=jax.ShapeDtypeStruct((ep_count * head_count, rows, width), BF),
        in_specs=[VMEM] * 5,
        out_specs=VMEM,
        scratch_shapes=[pltpu.VMEM((ep_count * rows, local_count * hidden_units), BF)],
        compiler_params=pltpu.CompilerParams(vmem_limit_bytes=8 << 20),
        cost_estimate=pl.CostEstimate(
            flops=ep_count * rows * weight_bytes, bytes_accessed=weight_bytes, transcendentals=0
        ),
        name="experts",
    )(
        in_vmem(gathered),
        in_vmem(gain_near),
        in_vmem(gate_weight),
        in_vmem(up_weight),
        in_vmem(down_weight),
    )
    arrived = lax.all_to_all(result, ("ep", "head"), 0, 0, tiled=True)
    local_sum = jnp.sum(arrived.astype(F32), 0).astype(BF)
    expert_sum = sum_over(local_sum, "side").astype(BF)
    return (after_attention, expert_sum)


def solution(mesh):
    placed = (
        P(("groups", "ep"), None),
        P(("groups", "ep"), "head", "side"),
        P(("groups", "ep"), "head"),
        P(("groups", "ep"), "head"),
        P(("groups", "ep"), None, "head"),
        P(("groups", "ep"), None, "head"),
        P(("groups", "ep")),
        P("head", "side", None),
        P(),
        P(("groups", "ep"), None),
        P(("groups", "ep"), None),
        P(("ep", "side"), None, "head"),
        P(("ep", "side"), None, "head"),
        P(("ep", "side"), "head", None),
    )
    return jax.shard_map(
        on_device,
        mesh=mesh,
        in_specs=placed,
        out_specs=(P(("groups", "ep"), "head"), P(("groups", "ep"), "head")),
        check_vma=False,
    )
```

```python
import functools
import math

import jax
import jax.numpy as jnp
from jax import lax
from jax.experimental import pallas as pl
from jax.experimental.pallas import tpu as pltpu
from jax.sharding import PartitionSpec as P

HD = 128
BF = jnp.bfloat16
F32 = jnp.float32
VMEM = pl.BlockSpec(memory_space=pltpu.VMEM)
HBM = pl.BlockSpec(memory_space=pltpu.HBM)


def in_vmem(x):
    return pltpu.with_memory_space_constraint(x, pltpu.VMEM)


def in_hbm(x):
    return pltpu.with_memory_space_constraint(x, pltpu.HBM)


def partners(count):
    steps = []
    k = 1
    while k < count:
        steps.append(k)
        k *= 2
    return steps


def swap(x, axis, k):
    count = lax.axis_size(axis)
    return lax.ppermute(x, axis, [(i, i ^ k) for i in range(count)])


def joint(x, axes, partner):
    sizes = [lax.axis_size(axis) for axis in axes]
    pairs = []
    for source in range(math.prod(sizes)):
        rest, place = source, []
        for size in reversed(sizes):
            place.insert(0, rest % size)
            rest //= size
        target = 0
        for size, index in zip(sizes, partner(*place)):
            target = target * size + index
        pairs.append((source, target))
    return lax.ppermute(x, axes, pairs)


def sum_heads(low):
    flip = min(lax.axis_size("side") - 1, 1)
    total = low.astype(F32)
    for k in partners(lax.axis_size("head")):
        low = total.astype(BF)
        other = joint(low, ("side", "head"), lambda s, h: (s ^ flip, h ^ k))
        total = low.astype(F32) + other.astype(F32)
    return total


def gather_rows(packed):
    ep_count, side_count = lax.axis_size("ep"), lax.axis_size("side")
    if (ep_count, side_count) == (4, 2):
        far = joint(packed, ("ep", "side"), lambda e, s: (e ^ (2 + s), s))
        near = joint(packed, ("ep", "side"), lambda e, s: (e ^ 1, s ^ 1))
        return jnp.concatenate([packed, near, far, swap(far, "side", 1)], 0)
    for k in partners(ep_count):
        packed = jnp.concatenate([packed, swap(packed, "ep", k)], 0)
    return packed


def source_of(block):
    me = lax.axis_index("ep")
    if (lax.axis_size("ep"), lax.axis_size("side")) == (4, 2) and block >= 2:
        side = lax.axis_index("side")
        return me ^ (block + side if block == 2 else block - side)
    return me ^ block


def sum_over(low, axis):
    total = low.astype(F32)
    for k in partners(lax.axis_size(axis)):
        low = total.astype(BF)
        total = low.astype(F32) + swap(low, axis, k).astype(F32)
    return total


def attend_kernel(
    lengths_hbm,
    query_hbm,
    new_key_hbm,
    new_value_hbm,
    cache_keys_hbm,
    cache_values_hbm,
    expert_ids_hbm,
    route_weights_hbm,
    hidden_hbm,
    norm_gain_hbm,
    out_weight_hbm,
    attended_out,
    coefficient_out,
    hidden_out,
    norm_gain_out,
    out_weight_out,
    lengths,
    query,
    new_key,
    new_value,
    cache_keys,
    cache_values,
    expert_ids,
    route_weights,
    arrivals,
):
    moves = [
        (lengths_hbm, lengths),
        (query_hbm, query),
        (cache_keys_hbm, cache_keys),
        (new_key_hbm, new_key),
        (new_value_hbm, new_value),
        (cache_values_hbm, cache_values),
        (expert_ids_hbm, expert_ids),
        (route_weights_hbm, route_weights),
        (hidden_hbm, hidden_out),
        (norm_gain_hbm, norm_gain_out),
        (out_weight_hbm, out_weight_out),
    ]
    copies = [
        pltpu.make_async_copy(source, target, arrivals.at[i])
        for i, (source, target) in enumerate(moves)
    ]
    for copy in copies:
        copy.start()
    rows, kv_local, width = query.shape
    context = cache_keys.shape[1]
    heads = width // HD
    total = rows * context
    scale = 1.0 / math.sqrt(HD)
    pairs = [(g, n) for g in range(kv_local) for n in range(heads)]
    for copy in copies[:4]:
        copy.wait()
    zero = jnp.zeros((rows, HD), BF)
    queries = [query[:, g, n * HD : (n + 1) * HD] for g, n in pairs]
    placed = [
        jnp.concatenate([q if g == other else zero for other in range(kv_local)], 1)
        for (g, n), q in zip(pairs, queries)
    ]
    stacked = jnp.concatenate(placed, 0)
    keys = cache_keys[...].reshape(total, kv_local * HD)
    contract = (((1,), (1,)), ((), ()))
    scores = lax.dot_general(stacked, keys, contract, preferred_element_type=F32) * scale
    scores = scores.reshape(len(pairs), rows, total)
    row = lax.broadcasted_iota(jnp.int32, (rows, total), 0)
    column = lax.broadcasted_iota(jnp.int32, (rows, total), 1)
    start = row * context
    end = start
    for r in range(rows):
        end = jnp.where(row == r, r * context + lengths[r], end)
    usable = (column >= start) & (column < end)
    scores = jnp.where(usable[None], scores, F32(-1e30))
    fresh = jnp.stack(
        [
            jnp.sum(
                q.astype(F32) * new_key[:, g * HD : (g + 1) * HD].astype(F32), 1, keepdims=True
            )
            for (g, n), q in zip(pairs, queries)
        ],
        0,
    ) * scale
    highest = jnp.maximum(jnp.max(scores, -1, keepdims=True), fresh)
    weights = jnp.exp(scores - highest)
    own = jnp.exp(fresh - highest)
    denominator = jnp.sum(weights, -1, keepdims=True) + own
    low = weights.astype(BF).reshape(len(pairs) * rows, total)
    for copy in copies[4:8]:
        copy.wait()
    values = cache_values[...].reshape(total, kv_local * HD)
    mixed = jnp.dot(low, values, preferred_element_type=F32)
    mixed = mixed.reshape(len(pairs), rows, kv_local * HD)
    own_low = own.astype(BF).astype(F32)
    for i, (g, n) in enumerate(pairs):
        block = slice(g * HD, (g + 1) * HD)
        value = mixed[i][:, block] + own_low[i] * new_value[:, block].astype(F32)
        attended_out[:, i * HD : (i + 1) * HD] = (value / denominator[i]).astype(BF)
    experts = coefficient_out.shape[1] // 2
    weight = route_weights[...]
    share = weight / jnp.sum(weight, 1, keepdims=True)
    lane = lax.broadcasted_iota(jnp.int32, (rows, experts), 1)
    coefficient = jnp.zeros((rows, experts), F32)
    for k in range(weight.shape[1]):
        coefficient += jnp.where(lane == expert_ids[:, k : k + 1], share[:, k : k + 1], F32(0.0))
    high = coefficient.astype(BF)
    rest = (coefficient - high.astype(F32)).astype(BF)
    coefficient_out[...] = jnp.concatenate([high, rest], 1)
    for copy in copies[8:]:
        copy.wait()


def project_kernel(attended, out_weight, hidden, partial_out):
    depth = out_weight.shape[2]
    projected = jnp.dot(
        attended[...],
        out_weight[...].reshape(attended.shape[1], depth),
        preferred_element_type=F32,
    )
    first = (lax.axis_index("side") == 0) & (lax.axis_index("head") == 0)
    base = jnp.where(first, hidden[...].astype(F32), F32(0.0))
    partial_out[...] = (projected + base).astype(BF)


def expert_kernel(
    gathered, norm_gain, gate_weight, up_weight, down_weight, out, inner, width
):
    count, depth, hidden_units = gate_weight.shape
    experts = (gathered.shape[1] - depth) // 2
    rows = gathered.shape[0]
    stream = gathered[:, :depth].astype(F32)
    norm = lax.rsqrt(jnp.mean(stream * stream, -1, keepdims=True) + 1e-06)
    normed = (stream * norm * norm_gain[...]).astype(BF)
    coefficient = gathered[:, depth : depth + experts].astype(F32) + gathered[
        :, depth + experts :
    ].astype(F32)
    lane = lax.broadcasted_iota(jnp.int32, (rows, experts), 1)
    me = lax.axis_index("ep")
    first = (me * lax.axis_size("side") + lax.axis_index("side")) * count
    for e in range(count):
        gate = jnp.dot(normed, gate_weight[e], preferred_element_type=F32)
        upper = jnp.dot(normed, up_weight[e], preferred_element_type=F32)
        share = jnp.sum(jnp.where(lane == first + e, coefficient, F32(0.0)), 1, keepdims=True)
        value = gate / (1.0 + jnp.exp(-gate)) * upper * share
        inner[:, e * hidden_units : (e + 1) * hidden_units] = value.astype(BF)
    result = jnp.dot(
        inner[...],
        down_weight[...].reshape(count * hidden_units, depth),
        preferred_element_type=F32,
    ).astype(BF)
    blocks, block_rows, _ = out.shape
    heads = depth // width
    for j in range(blocks // heads):
        target = source_of(j)
        for h in range(heads):
            out[target * heads + h] = result[
                j * block_rows : (j + 1) * block_rows, h * width : (h + 1) * width
            ]


def on_device(
    hidden,
    query,
    new_key,
    new_value,
    cache_keys,
    cache_values,
    lengths,
    out_weight,
    norm_gain,
    expert_ids,
    route_weights,
    gate_weight,
    up_weight,
    down_weight,
):
    ep_count = lax.axis_size("ep")
    side_count = lax.axis_size("side")
    head_count = lax.axis_size("head")
    head_index = lax.axis_index("head")
    rows, depth = hidden.shape
    local_count, _, hidden_units = gate_weight.shape
    experts = local_count * ep_count * side_count
    width = depth // head_count
    top = expert_ids.shape[1]
    gain = norm_gain.reshape(1, depth)
    attended, coefficient, hidden_near, gain_near, out_weight_near = pl.pallas_call(
        attend_kernel,
        out_shape=(
            pltpu.VMEM((rows, out_weight.shape[0] * out_weight.shape[1]), BF),
            pltpu.VMEM((rows, 2 * experts), BF),
            pltpu.VMEM(hidden.shape, BF),
            pltpu.VMEM(gain.shape, F32),
            pltpu.VMEM(out_weight.shape, BF),
        ),
        in_specs=[HBM] * 11,
        out_specs=(VMEM,) * 5,
        scratch_shapes=[
            pltpu.SMEM(lengths.shape, jnp.int32),
            pltpu.VMEM(query.shape, BF),
            pltpu.VMEM(new_key.shape, BF),
            pltpu.VMEM(new_value.shape, BF),
            pltpu.VMEM(cache_keys.shape, BF),
            pltpu.VMEM(cache_values.shape, BF),
            pltpu.VMEM((rows, top), jnp.int32),
            pltpu.VMEM((rows, top), F32),
            pltpu.SemaphoreType.DMA((11,)),
        ],
        compiler_params=pltpu.CompilerParams(vmem_limit_bytes=8 << 20),
        name="attend",
    )(
        in_hbm(lengths),
        in_hbm(query),
        in_hbm(new_key),
        in_hbm(new_value),
        in_hbm(cache_keys),
        in_hbm(cache_values),
        in_hbm(expert_ids),
        in_hbm(route_weights),
        in_hbm(hidden),
        in_hbm(gain),
        in_hbm(out_weight),
    )
    partial_value = pl.pallas_call(
        project_kernel,
        out_shape=pltpu.VMEM((rows, depth), BF),
        in_specs=[VMEM] * 3,
        out_specs=VMEM,
        compiler_params=pltpu.CompilerParams(vmem_limit_bytes=8 << 20),
        cost_estimate=pl.CostEstimate(
            flops=10**12, bytes_accessed=200 * 10**6, transcendentals=0
        ),
        name="project",
    )(in_vmem(attended), in_vmem(out_weight_near), in_vmem(hidden_near))
    stream = sum_heads(sum_over(partial_value, "side").astype(BF))
    after_attention = lax.dynamic_slice_in_dim(stream, head_index * width, width, 1)
    packed = jnp.concatenate([stream.astype(BF), coefficient], 1)
    gathered = gather_rows(packed)
    weight_bytes = 2 * (gate_weight.size + up_weight.size + down_weight.size)
    result = pl.pallas_call(
        functools.partial(expert_kernel, width=width),
        out_shape=jax.ShapeDtypeStruct((ep_count * head_count, rows, width), BF),
        in_specs=[VMEM] * 5,
        out_specs=VMEM,
        scratch_shapes=[pltpu.VMEM((ep_count * rows, local_count * hidden_units), BF)],
        compiler_params=pltpu.CompilerParams(vmem_limit_bytes=8 << 20),
        cost_estimate=pl.CostEstimate(
            flops=ep_count * rows * weight_bytes, bytes_accessed=weight_bytes, transcendentals=0
        ),
        name="experts",
    )(
        in_vmem(gathered),
        in_vmem(gain_near),
        in_vmem(gate_weight),
        in_vmem(up_weight),
        in_vmem(down_weight),
    )
    arrived = lax.all_to_all(result, ("ep", "head"), 0, 0, tiled=True)
    local_sum = jnp.sum(arrived.astype(F32), 0).astype(BF)
    expert_sum = sum_over(local_sum, "side").astype(BF)
    return (after_attention, expert_sum)


def solution(mesh):
    placed = (
        P(("groups", "ep"), None),
        P(("groups", "ep"), "head", "side"),
        P(("groups", "ep"), "head"),
        P(("groups", "ep"), "head"),
        P(("groups", "ep"), None, "head"),
        P(("groups", "ep"), None, "head"),
        P(("groups", "ep")),
        P("head", "side", None),
        P(),
        P(("groups", "ep"), None),
        P(("groups", "ep"), None),
        P(("ep", "side"), None, "head"),
        P(("ep", "side"), None, "head"),
        P(("ep", "side"), "head", None),
    )
    return jax.shard_map(
        on_device,
        mesh=mesh,
        in_specs=placed,
        out_specs=(P(("groups", "ep"), "head"), P(("groups", "ep"), "head")),
        check_vma=False,
    )
```

```python
import functools
import math

import jax
import jax.numpy as jnp
from jax import lax
from jax.experimental import pallas as pl
from jax.experimental.pallas import tpu as pltpu
from jax.sharding import PartitionSpec as P

HD = 128
BF = jnp.bfloat16
F32 = jnp.float32
VMEM = pl.BlockSpec(memory_space=pltpu.VMEM)
HBM = pl.BlockSpec(memory_space=pltpu.HBM)


def in_vmem(x):
    return pltpu.with_memory_space_constraint(x, pltpu.VMEM)


def in_hbm(x):
    return pltpu.with_memory_space_constraint(x, pltpu.HBM)


def partners(count):
    steps = []
    k = 1
    while k < count:
        steps.append(k)
        k *= 2
    return steps


def swap(x, axis, k):
    count = lax.axis_size(axis)
    return lax.ppermute(x, axis, [(i, i ^ k) for i in range(count)])


def joint(x, axes, partner):
    sizes = [lax.axis_size(axis) for axis in axes]
    pairs = []
    for source in range(math.prod(sizes)):
        rest, place = source, []
        for size in reversed(sizes):
            place.insert(0, rest % size)
            rest //= size
        target = 0
        for size, index in zip(sizes, partner(*place)):
            target = target * size + index
        pairs.append((source, target))
    return lax.ppermute(x, axes, pairs)


def sum_heads(low):
    flip = min(lax.axis_size("side") - 1, 1)
    total = low.astype(F32)
    for k in partners(lax.axis_size("head")):
        low = total.astype(BF)
        other = joint(low, ("side", "head"), lambda s, h: (s ^ flip, h ^ k))
        total = low.astype(F32) + other.astype(F32)
    return total


def gather_rows(packed):
    ep_count, side_count = lax.axis_size("ep"), lax.axis_size("side")
    if (ep_count, side_count) == (4, 2):
        far = joint(packed, ("ep", "side"), lambda e, s: (e ^ (2 + s), s))
        near = joint(packed, ("ep", "side"), lambda e, s: (e ^ 1, s ^ 1))
        return jnp.concatenate([packed, near, far, swap(far, "side", 1)], 0)
    for k in partners(ep_count):
        packed = jnp.concatenate([packed, swap(packed, "ep", k)], 0)
    return packed


def source_of(block):
    me = lax.axis_index("ep")
    if (lax.axis_size("ep"), lax.axis_size("side")) == (4, 2) and block >= 2:
        side = lax.axis_index("side")
        return me ^ (block + side if block == 2 else block - side)
    return me ^ block


def sum_over(low, axis):
    total = low.astype(F32)
    for k in partners(lax.axis_size(axis)):
        low = total.astype(BF)
        total = low.astype(F32) + swap(low, axis, k).astype(F32)
    return total


def attend_kernel(
    lengths_hbm,
    query_hbm,
    new_key_hbm,
    new_value_hbm,
    cache_keys_hbm,
    cache_values_hbm,
    expert_ids_hbm,
    route_weights_hbm,
    hidden_hbm,
    norm_gain_hbm,
    out_weight_hbm,
    partial_out,
    coefficient_out,
    norm_gain_out,
    lengths,
    query,
    new_key,
    new_value,
    cache_keys,
    cache_values,
    expert_ids,
    route_weights,
    hidden,
    out_weight,
    arrivals,
    weight_arrivals,
):
    moves = [
        (lengths_hbm, lengths),
        (query_hbm, query),
        (cache_keys_hbm, cache_keys),
        (new_key_hbm, new_key),
        (new_value_hbm, new_value),
        (cache_values_hbm, cache_values),
        (expert_ids_hbm, expert_ids),
        (route_weights_hbm, route_weights),
        (hidden_hbm, hidden),
        (norm_gain_hbm, norm_gain_out),
    ]
    copies = [
        pltpu.make_async_copy(source, target, arrivals.at[i])
        for i, (source, target) in enumerate(moves)
    ]
    rows, kv_local, width = query.shape
    depth = out_weight.shape[2]
    step = math.gcd(width, 2 * HD)
    pieces = [(g, c) for g in range(kv_local) for c in range(0, width, step)]
    weight_copies = [
        pltpu.make_async_copy(
            out_weight_hbm.at[g, pl.ds(c, step)],
            out_weight.at[g, pl.ds(c, step)],
            weight_arrivals.at[i],
        )
        for i, (g, c) in enumerate(pieces)
    ]
    for copy in copies + weight_copies:
        copy.start()
    context = cache_keys.shape[1]
    heads = width // HD
    total = rows * context
    scale = 1.0 / math.sqrt(HD)
    pairs = [(g, n) for g in range(kv_local) for n in range(heads)]
    for copy in copies[:4]:
        copy.wait()
    zero = jnp.zeros((rows, HD), BF)
    queries = [query[:, g, n * HD : (n + 1) * HD] for g, n in pairs]
    placed = [
        jnp.concatenate([q if g == other else zero for other in range(kv_local)], 1)
        for (g, n), q in zip(pairs, queries)
    ]
    stacked = jnp.concatenate(placed, 0)
    keys = cache_keys[...].reshape(total, kv_local * HD)
    contract = (((1,), (1,)), ((), ()))
    scores = lax.dot_general(stacked, keys, contract, preferred_element_type=F32) * scale
    scores = scores.reshape(len(pairs), rows, total)
    row = lax.broadcasted_iota(jnp.int32, (rows, total), 0)
    column = lax.broadcasted_iota(jnp.int32, (rows, total), 1)
    start = row * context
    end = start
    for r in range(rows):
        end = jnp.where(row == r, r * context + lengths[r], end)
    usable = (column >= start) & (column < end)
    scores = jnp.where(usable[None], scores, F32(-1e30))
    fresh = jnp.stack(
        [
            jnp.sum(
                q.astype(F32) * new_key[:, g * HD : (g + 1) * HD].astype(F32), 1, keepdims=True
            )
            for (g, n), q in zip(pairs, queries)
        ],
        0,
    ) * scale
    highest = jnp.maximum(jnp.max(scores, -1, keepdims=True), fresh)
    weights = jnp.exp(scores - highest)
    own = jnp.exp(fresh - highest)
    denominator = jnp.sum(weights, -1, keepdims=True) + own
    low = weights.astype(BF).reshape(len(pairs) * rows, total)
    for copy in copies[4:8]:
        copy.wait()
    values = cache_values[...].reshape(total, kv_local * HD)
    mixed = jnp.dot(low, values, preferred_element_type=F32)
    mixed = mixed.reshape(len(pairs), rows, kv_local * HD)
    own_low = own.astype(BF).astype(F32)
    attended = []
    for i, (g, n) in enumerate(pairs):
        block = slice(g * HD, (g + 1) * HD)
        value = mixed[i][:, block] + own_low[i] * new_value[:, block].astype(F32)
        attended.append((value / denominator[i]).astype(BF))
    attended = jnp.concatenate(attended, 1)
    experts = coefficient_out.shape[1] // 2
    weight = route_weights[...]
    share = weight / jnp.sum(weight, 1, keepdims=True)
    lane = lax.broadcasted_iota(jnp.int32, (rows, experts), 1)
    coefficient = jnp.zeros((rows, experts), F32)
    for k in range(weight.shape[1]):
        coefficient += jnp.where(lane == expert_ids[:, k : k + 1], share[:, k : k + 1], F32(0.0))
    high = coefficient.astype(BF)
    rest = (coefficient - high.astype(F32)).astype(BF)
    coefficient_out[...] = jnp.concatenate([high, rest], 1)
    for copy in copies[8:]:
        copy.wait()
    first = (lax.axis_index("side") == 0) & (lax.axis_index("head") == 0)
    projected = jnp.where(first, hidden[...].astype(F32), F32(0.0))
    for copy, (g, c) in zip(weight_copies, pieces):
        copy.wait()
        low = g * width + c
        projected += jnp.dot(
            attended[:, low : low + step], out_weight[g, c : c + step], preferred_element_type=F32
        )
    partial_out[...] = projected.astype(BF)


def add_kernel(mine, other, out):
    out[...] = (mine[...].astype(F32) + other[...].astype(F32)).astype(BF)


def expert_kernel(
    gathered, norm_gain, gate_weight, up_weight, down_weight_hbm, out, inner, total, down_weight, arrivals, width
):
    count, depth, hidden_units = gate_weight.shape
    experts = (gathered.shape[1] - depth) // 2
    rows = gathered.shape[0]
    copies = [
        pltpu.make_async_copy(down_weight_hbm.at[e], down_weight.at[e], arrivals.at[e])
        for e in range(count)
    ]
    for copy in copies:
        copy.start()
    stream = gathered[:, :depth].astype(F32)
    norm = lax.rsqrt(jnp.mean(stream * stream, -1, keepdims=True) + 1e-06)
    normed = (stream * norm * norm_gain[...]).astype(BF)
    coefficient = gathered[:, depth : depth + experts].astype(F32) + gathered[
        :, depth + experts :
    ].astype(F32)
    lane = lax.broadcasted_iota(jnp.int32, (rows, experts), 1)
    me = lax.axis_index("ep")
    first = (me * lax.axis_size("side") + lax.axis_index("side")) * count
    for e in range(count):
        gate = jnp.dot(normed, gate_weight[e], preferred_element_type=F32)
        upper = jnp.dot(normed, up_weight[e], preferred_element_type=F32)
        share = jnp.sum(jnp.where(lane == first + e, coefficient, F32(0.0)), 1, keepdims=True)
        value = gate / (1.0 + jnp.exp(-gate)) * upper * share
        inner[:, e * hidden_units : (e + 1) * hidden_units] = value.astype(BF)
    group = 2 if count % 2 == 0 else 1
    for low in range(0, count, group):
        for copy in copies[low : low + group]:
            copy.wait()
        part = jnp.dot(
            inner[:, low * hidden_units : (low + group) * hidden_units],
            down_weight[low : low + group].reshape(group * hidden_units, depth),
            preferred_element_type=F32,
        )
        if low == 0:
            total[...] = part
        else:
            total[...] += part
    result = total[...].astype(BF)
    blocks, block_rows, _ = out.shape
    heads = depth // width
    for j in range(blocks // heads):
        target = source_of(j)
        for h in range(heads):
            out[target * heads + h] = result[
                j * block_rows : (j + 1) * block_rows, h * width : (h + 1) * width
            ]


def run_experts(gathered, gain, gate_weight, up_weight, down_weight, head_count, ep_count):
    local_count, depth, hidden_units = gate_weight.shape
    rows = gathered.shape[0] // ep_count
    width = depth // head_count
    weight_bytes = 2 * (gate_weight.size + up_weight.size + down_weight.size)
    return pl.pallas_call(
        functools.partial(expert_kernel, width=width),
        out_shape=jax.ShapeDtypeStruct((ep_count * head_count, rows, width), BF),
        in_specs=[VMEM] * 4 + [HBM],
        out_specs=VMEM,
        scratch_shapes=[
            pltpu.VMEM((ep_count * rows, local_count * hidden_units), BF),
            pltpu.VMEM((ep_count * rows, depth), F32),
            pltpu.VMEM(down_weight.shape, BF),
            pltpu.SemaphoreType.DMA((local_count,)),
        ],
        compiler_params=pltpu.CompilerParams(vmem_limit_bytes=24 << 20),
        cost_estimate=pl.CostEstimate(
            flops=ep_count * rows * weight_bytes, bytes_accessed=weight_bytes, transcendentals=0
        ),
        name="experts",
    )(
        in_vmem(gathered),
        in_vmem(gain),
        in_vmem(gate_weight),
        in_vmem(up_weight),
        in_hbm(down_weight),
    )


def on_device(
    hidden,
    query,
    new_key,
    new_value,
    cache_keys,
    cache_values,
    lengths,
    out_weight,
    norm_gain,
    expert_ids,
    route_weights,
    gate_weight,
    up_weight,
    down_weight,
):
    ep_count = lax.axis_size("ep")
    side_count = lax.axis_size("side")
    head_count = lax.axis_size("head")
    head_index = lax.axis_index("head")
    rows, depth = hidden.shape
    local_count, _, hidden_units = gate_weight.shape
    experts = local_count * ep_count * side_count
    width = depth // head_count
    top = expert_ids.shape[1]
    gain = norm_gain.reshape(1, depth)
    pieces = out_weight.shape[0] * (out_weight.shape[1] // math.gcd(out_weight.shape[1], 2 * HD))
    partial_value, coefficient, gain_near = pl.pallas_call(
        attend_kernel,
        out_shape=(
            pltpu.VMEM((rows, depth), BF),
            pltpu.VMEM((rows, 2 * experts), BF),
            pltpu.VMEM(gain.shape, F32),
        ),
        in_specs=[HBM] * 11,
        out_specs=(VMEM,) * 3,
        scratch_shapes=[
            pltpu.SMEM(lengths.shape, jnp.int32),
            pltpu.VMEM(query.shape, BF),
            pltpu.VMEM(new_key.shape, BF),
            pltpu.VMEM(new_value.shape, BF),
            pltpu.VMEM(cache_keys.shape, BF),
            pltpu.VMEM(cache_values.shape, BF),
            pltpu.VMEM((rows, top), jnp.int32),
            pltpu.VMEM((rows, top), F32),
            pltpu.VMEM(hidden.shape, BF),
            pltpu.VMEM(out_weight.shape, BF),
            pltpu.SemaphoreType.DMA((10,)),
            pltpu.SemaphoreType.DMA((pieces,)),
        ],
        compiler_params=pltpu.CompilerParams(vmem_limit_bytes=16 << 20),
        name="attend",
    )(
        in_hbm(lengths),
        in_hbm(query),
        in_hbm(new_key),
        in_hbm(new_value),
        in_hbm(cache_keys),
        in_hbm(cache_values),
        in_hbm(expert_ids),
        in_hbm(route_weights),
        in_hbm(hidden),
        in_hbm(gain),
        in_hbm(out_weight),
    )
    for k in partners(side_count):
        other = swap(partial_value, "side", k)
        partial_value = pl.pallas_call(
            add_kernel,
            out_shape=pltpu.VMEM((rows, depth), BF),
            in_specs=[VMEM] * 2,
            out_specs=VMEM,
            compiler_params=pltpu.CompilerParams(vmem_limit_bytes=4 << 20),
            cost_estimate=pl.CostEstimate(
                flops=10**12, bytes_accessed=200 * 10**6, transcendentals=0
            ),
            name="side_sum",
        )(in_vmem(partial_value), in_vmem(other))
    stream = sum_heads(partial_value)
    after_attention = lax.dynamic_slice_in_dim(stream, head_index * width, width, 1)
    packed = jnp.concatenate([stream.astype(BF), coefficient], 1)
    gathered = gather_rows(packed)
    result = run_experts(
        gathered, gain_near, gate_weight, up_weight, down_weight, head_count, ep_count
    )
    arrived = lax.all_to_all(result, ("ep", "head"), 0, 0, tiled=True)
    local_sum = jnp.sum(arrived.astype(F32), 0).astype(BF)
    expert_sum = sum_over(local_sum, "side").astype(BF)
    return (after_attention, expert_sum)


def solution(mesh):
    placed = (
        P(("groups", "ep"), None),
        P(("groups", "ep"), "head", "side"),
        P(("groups", "ep"), "head"),
        P(("groups", "ep"), "head"),
        P(("groups", "ep"), None, "head"),
        P(("groups", "ep"), None, "head"),
        P(("groups", "ep")),
        P("head", "side", None),
        P(),
        P(("groups", "ep"), None),
        P(("groups", "ep"), None),
        P(("ep", "side"), None, "head"),
        P(("ep", "side"), None, "head"),
        P(("ep", "side"), "head", None),
    )
    return jax.shard_map(
        on_device,
        mesh=mesh,
        in_specs=placed,
        out_specs=(P(("groups", "ep"), "head"), P(("groups", "ep"), "head")),
        check_vma=False,
    )
```

```python
import functools
import math

import jax
import jax.numpy as jnp
from jax import lax
from jax.experimental import pallas as pl
from jax.experimental.pallas import tpu as pltpu
from jax.sharding import PartitionSpec as P

HD = 128
BF = jnp.bfloat16
F32 = jnp.float32
VMEM = pl.BlockSpec(memory_space=pltpu.VMEM)
HBM = pl.BlockSpec(memory_space=pltpu.HBM)


def in_vmem(x):
    return pltpu.with_memory_space_constraint(x, pltpu.VMEM)


def in_hbm(x):
    return pltpu.with_memory_space_constraint(x, pltpu.HBM)


def partners(count):
    steps = []
    k = 1
    while k < count:
        steps.append(k)
        k *= 2
    return steps


def swap(x, axis, k):
    count = lax.axis_size(axis)
    return lax.ppermute(x, axis, [(i, i ^ k) for i in range(count)])


def joint(x, axes, partner):
    sizes = [lax.axis_size(axis) for axis in axes]
    pairs = []
    for source in range(math.prod(sizes)):
        rest, place = source, []
        for size in reversed(sizes):
            place.insert(0, rest % size)
            rest //= size
        target = 0
        for size, index in zip(sizes, partner(*place)):
            target = target * size + index
        pairs.append((source, target))
    return lax.ppermute(x, axes, pairs)


def sum_heads(low):
    flip = min(lax.axis_size("side") - 1, 1)
    total = low.astype(F32)
    for k in partners(lax.axis_size("head")):
        low = total.astype(BF)
        other = joint(low, ("side", "head"), lambda s, h: (s ^ flip, h ^ k))
        total = low.astype(F32) + other.astype(F32)
    return total


def gather_rows(packed):
    ep_count, side_count = lax.axis_size("ep"), lax.axis_size("side")
    if (ep_count, side_count) == (4, 2):
        far = joint(packed, ("ep", "side"), lambda e, s: (e ^ (2 + s), s))
        near = joint(packed, ("ep", "side"), lambda e, s: (e ^ 1, s ^ 1))
        return jnp.concatenate([packed, near, far, swap(far, "side", 1)], 0)
    for k in partners(ep_count):
        packed = jnp.concatenate([packed, swap(packed, "ep", k)], 0)
    return packed


def source_of(block):
    me = lax.axis_index("ep")
    if (lax.axis_size("ep"), lax.axis_size("side")) == (4, 2) and block >= 2:
        side = lax.axis_index("side")
        return me ^ (block + side if block == 2 else block - side)
    return me ^ block


def sum_over(low, axis):
    total = low.astype(F32)
    for k in partners(lax.axis_size(axis)):
        low = total.astype(BF)
        total = low.astype(F32) + swap(low, axis, k).astype(F32)
    return total


def attend_kernel(
    lengths_hbm,
    query_hbm,
    new_key_hbm,
    new_value_hbm,
    cache_keys_hbm,
    cache_values_hbm,
    expert_ids_hbm,
    route_weights_hbm,
    hidden_hbm,
    norm_gain_hbm,
    out_weight_hbm,
    partial_out,
    coefficient_out,
    norm_gain_out,
    lengths,
    query,
    new_key,
    new_value,
    cache_keys,
    cache_values,
    expert_ids,
    route_weights,
    hidden,
    out_weight,
    arrivals,
    weight_arrivals,
):
    moves = [
        (lengths_hbm, lengths),
        (query_hbm, query),
        (cache_keys_hbm, cache_keys),
        (new_key_hbm, new_key),
        (new_value_hbm, new_value),
        (cache_values_hbm, cache_values),
        (expert_ids_hbm, expert_ids),
        (route_weights_hbm, route_weights),
        (hidden_hbm, hidden),
        (norm_gain_hbm, norm_gain_out),
    ]
    copies = [
        pltpu.make_async_copy(source, target, arrivals.at[i])
        for i, (source, target) in enumerate(moves)
    ]
    rows, kv_local, width = query.shape
    depth = out_weight.shape[2]
    step = math.gcd(width, 2 * HD)
    pieces = [(g, c) for g in range(kv_local) for c in range(0, width, step)]
    weight_copies = [
        pltpu.make_async_copy(
            out_weight_hbm.at[g, pl.ds(c, step)],
            out_weight.at[g, pl.ds(c, step)],
            weight_arrivals.at[i],
        )
        for i, (g, c) in enumerate(pieces)
    ]
    for copy in copies + weight_copies:
        copy.start()
    context = cache_keys.shape[1]
    heads = width // HD
    total = rows * context
    scale = 1.0 / math.sqrt(HD)
    pairs = [(g, n) for g in range(kv_local) for n in range(heads)]
    for copy in copies[:4]:
        copy.wait()
    zero = jnp.zeros((rows, HD), BF)
    queries = [query[:, g, n * HD : (n + 1) * HD] for g, n in pairs]
    placed = [
        jnp.concatenate([q if g == other else zero for other in range(kv_local)], 1)
        for (g, n), q in zip(pairs, queries)
    ]
    stacked = jnp.concatenate(placed, 0)
    keys = cache_keys[...].reshape(total, kv_local * HD)
    contract = (((1,), (1,)), ((), ()))
    scores = lax.dot_general(stacked, keys, contract, preferred_element_type=F32) * scale
    scores = scores.reshape(len(pairs), rows, total)
    row = lax.broadcasted_iota(jnp.int32, (rows, total), 0)
    column = lax.broadcasted_iota(jnp.int32, (rows, total), 1)
    start = row * context
    end = start
    for r in range(rows):
        end = jnp.where(row == r, r * context + lengths[r], end)
    usable = (column >= start) & (column < end)
    scores = jnp.where(usable[None], scores, F32(-1e30))
    fresh = jnp.stack(
        [
            jnp.sum(
                q.astype(F32) * new_key[:, g * HD : (g + 1) * HD].astype(F32), 1, keepdims=True
            )
            for (g, n), q in zip(pairs, queries)
        ],
        0,
    ) * scale
    highest = jnp.maximum(jnp.max(scores, -1, keepdims=True), fresh)
    weights = jnp.exp(scores - highest)
    own = jnp.exp(fresh - highest)
    denominator = jnp.sum(weights, -1, keepdims=True) + own
    low = weights.astype(BF).reshape(len(pairs) * rows, total)
    for copy in copies[4:8]:
        copy.wait()
    values = cache_values[...].reshape(total, kv_local * HD)
    mixed = jnp.dot(low, values, preferred_element_type=F32)
    mixed = mixed.reshape(len(pairs), rows, kv_local * HD)
    own_low = own.astype(BF).astype(F32)
    attended = []
    for i, (g, n) in enumerate(pairs):
        block = slice(g * HD, (g + 1) * HD)
        value = mixed[i][:, block] + own_low[i] * new_value[:, block].astype(F32)
        attended.append((value / denominator[i]).astype(BF))
    attended = jnp.concatenate(attended, 1)
    experts = coefficient_out.shape[1] // 2
    weight = route_weights[...]
    share = weight / jnp.sum(weight, 1, keepdims=True)
    lane = lax.broadcasted_iota(jnp.int32, (rows, experts), 1)
    coefficient = jnp.zeros((rows, experts), F32)
    for k in range(weight.shape[1]):
        coefficient += jnp.where(lane == expert_ids[:, k : k + 1], share[:, k : k + 1], F32(0.0))
    high = coefficient.astype(BF)
    rest = (coefficient - high.astype(F32)).astype(BF)
    coefficient_out[...] = jnp.concatenate([high, rest], 1)
    for copy in copies[8:]:
        copy.wait()
    first = (lax.axis_index("side") == 0) & (lax.axis_index("head") == 0)
    projected = jnp.where(first, hidden[...].astype(F32), F32(0.0))
    for copy, (g, c) in zip(weight_copies, pieces):
        copy.wait()
        low = g * width + c
        projected += jnp.dot(
            attended[:, low : low + step], out_weight[g, c : c + step], preferred_element_type=F32
        )
    partial_out[...] = projected.astype(BF)


def add_kernel(mine, other, out):
    out[...] = (mine[...].astype(F32) + other[...].astype(F32)).astype(BF)


def expert_kernel(
    gathered, norm_gain, gate_weight, up_weight, down_weight, out, inner, width
):
    count, depth, hidden_units = gate_weight.shape
    experts = (gathered.shape[1] - depth) // 2
    rows = gathered.shape[0]
    stream = gathered[:, :depth].astype(F32)
    norm = lax.rsqrt(jnp.mean(stream * stream, -1, keepdims=True) + 1e-06)
    normed = (stream * norm * norm_gain[...]).astype(BF)
    coefficient = gathered[:, depth : depth + experts].astype(F32) + gathered[
        :, depth + experts :
    ].astype(F32)
    lane = lax.broadcasted_iota(jnp.int32, (rows, experts), 1)
    me = lax.axis_index("ep")
    first = (me * lax.axis_size("side") + lax.axis_index("side")) * count
    for e in range(count):
        gate = jnp.dot(normed, gate_weight[e], preferred_element_type=F32)
        upper = jnp.dot(normed, up_weight[e], preferred_element_type=F32)
        share = jnp.sum(jnp.where(lane == first + e, coefficient, F32(0.0)), 1, keepdims=True)
        value = gate / (1.0 + jnp.exp(-gate)) * upper * share
        inner[:, e * hidden_units : (e + 1) * hidden_units] = value.astype(BF)
    result = jnp.dot(
        inner[...],
        down_weight[...].reshape(count * hidden_units, depth),
        preferred_element_type=F32,
    ).astype(BF)
    blocks, block_rows, _ = out.shape
    heads = depth // width
    for j in range(blocks // heads):
        target = source_of(j)
        for h in range(heads):
            out[target * heads + h] = result[
                j * block_rows : (j + 1) * block_rows, h * width : (h + 1) * width
            ]


def run_experts(gathered, gain, gate_weight, up_weight, down_weight, head_count, ep_count):
    local_count, depth, hidden_units = gate_weight.shape
    rows = gathered.shape[0] // ep_count
    width = depth // head_count
    weight_bytes = 2 * (gate_weight.size + up_weight.size + down_weight.size)
    return pl.pallas_call(
        functools.partial(expert_kernel, width=width),
        out_shape=jax.ShapeDtypeStruct((ep_count * head_count, rows, width), BF),
        in_specs=[VMEM] * 5,
        out_specs=VMEM,
        scratch_shapes=[
            pltpu.VMEM((ep_count * rows, local_count * hidden_units), BF),
        ],
        compiler_params=pltpu.CompilerParams(vmem_limit_bytes=8 << 20),
        cost_estimate=pl.CostEstimate(
            flops=ep_count * rows * weight_bytes, bytes_accessed=weight_bytes, transcendentals=0
        ),
        name="experts",
    )(
        in_vmem(gathered),
        in_vmem(gain),
        in_vmem(gate_weight),
        in_vmem(up_weight),
        in_vmem(down_weight),
    )


def on_device(
    hidden,
    query,
    new_key,
    new_value,
    cache_keys,
    cache_values,
    lengths,
    out_weight,
    norm_gain,
    expert_ids,
    route_weights,
    gate_weight,
    up_weight,
    down_weight,
):
    ep_count = lax.axis_size("ep")
    side_count = lax.axis_size("side")
    head_count = lax.axis_size("head")
    head_index = lax.axis_index("head")
    rows, depth = hidden.shape
    local_count, _, hidden_units = gate_weight.shape
    experts = local_count * ep_count * side_count
    width = depth // head_count
    top = expert_ids.shape[1]
    gain = norm_gain.reshape(1, depth)
    pieces = out_weight.shape[0] * (out_weight.shape[1] // math.gcd(out_weight.shape[1], 2 * HD))
    partial_value, coefficient, gain_near = pl.pallas_call(
        attend_kernel,
        out_shape=(
            pltpu.VMEM((rows, depth), BF),
            pltpu.VMEM((rows, 2 * experts), BF),
            pltpu.VMEM(gain.shape, F32),
        ),
        in_specs=[HBM] * 11,
        out_specs=(VMEM,) * 3,
        scratch_shapes=[
            pltpu.SMEM(lengths.shape, jnp.int32),
            pltpu.VMEM(query.shape, BF),
            pltpu.VMEM(new_key.shape, BF),
            pltpu.VMEM(new_value.shape, BF),
            pltpu.VMEM(cache_keys.shape, BF),
            pltpu.VMEM(cache_values.shape, BF),
            pltpu.VMEM((rows, top), jnp.int32),
            pltpu.VMEM((rows, top), F32),
            pltpu.VMEM(hidden.shape, BF),
            pltpu.VMEM(out_weight.shape, BF),
            pltpu.SemaphoreType.DMA((10,)),
            pltpu.SemaphoreType.DMA((pieces,)),
        ],
        compiler_params=pltpu.CompilerParams(vmem_limit_bytes=16 << 20),
        cost_estimate=pl.CostEstimate(
            flops=10**12, bytes_accessed=200 * 10**6, transcendentals=0
        ),
        name="attend",
    )(
        in_hbm(lengths),
        in_hbm(query),
        in_hbm(new_key),
        in_hbm(new_value),
        in_hbm(cache_keys),
        in_hbm(cache_values),
        in_hbm(expert_ids),
        in_hbm(route_weights),
        in_hbm(hidden),
        in_hbm(gain),
        in_hbm(out_weight),
    )
    for k in partners(side_count):
        other = swap(partial_value, "side", k)
        partial_value = pl.pallas_call(
            add_kernel,
            out_shape=pltpu.VMEM((rows, depth), BF),
            in_specs=[VMEM] * 2,
            out_specs=VMEM,
            compiler_params=pltpu.CompilerParams(vmem_limit_bytes=4 << 20),
            name="side_sum",
        )(in_vmem(partial_value), in_vmem(other))
    stream = sum_heads(partial_value)
    after_attention = lax.dynamic_slice_in_dim(stream, head_index * width, width, 1)
    packed = jnp.concatenate([stream.astype(BF), coefficient], 1)
    gathered = gather_rows(packed)
    result = run_experts(
        gathered, gain_near, gate_weight, up_weight, down_weight, head_count, ep_count
    )
    arrived = lax.all_to_all(result, ("ep", "head"), 0, 0, tiled=True)
    local_sum = jnp.sum(arrived.astype(F32), 0).astype(BF)
    expert_sum = sum_over(local_sum, "side").astype(BF)
    return (after_attention, expert_sum)


def solution(mesh):
    placed = (
        P(("groups", "ep"), None),
        P(("groups", "ep"), "head", "side"),
        P(("groups", "ep"), "head"),
        P(("groups", "ep"), "head"),
        P(("groups", "ep"), None, "head"),
        P(("groups", "ep"), None, "head"),
        P(("groups", "ep")),
        P("head", "side", None),
        P(),
        P(("groups", "ep"), None),
        P(("groups", "ep"), None),
        P(("ep", "side"), None, "head"),
        P(("ep", "side"), None, "head"),
        P(("ep", "side"), "head", None),
    )
    return jax.shard_map(
        on_device,
        mesh=mesh,
        in_specs=placed,
        out_specs=(P(("groups", "ep"), "head"), P(("groups", "ep"), "head")),
        check_vma=False,
    )
```

```python
import functools
import math

import jax
import jax.numpy as jnp
from jax import lax
from jax.experimental import pallas as pl
from jax.experimental.pallas import tpu as pltpu
from jax.sharding import PartitionSpec as P

HD = 128
BF = jnp.bfloat16
F32 = jnp.float32
VMEM = pl.BlockSpec(memory_space=pltpu.VMEM)
HBM = pl.BlockSpec(memory_space=pltpu.HBM)


def in_vmem(x):
    return pltpu.with_memory_space_constraint(x, pltpu.VMEM)


def in_hbm(x):
    return pltpu.with_memory_space_constraint(x, pltpu.HBM)


def partners(count):
    steps = []
    k = 1
    while k < count:
        steps.append(k)
        k *= 2
    return steps


def swap(x, axis, k):
    count = lax.axis_size(axis)
    return lax.ppermute(x, axis, [(i, i ^ k) for i in range(count)])


def joint(x, axes, partner):
    sizes = [lax.axis_size(axis) for axis in axes]
    pairs = []
    for source in range(math.prod(sizes)):
        rest, place = source, []
        for size in reversed(sizes):
            place.insert(0, rest % size)
            rest //= size
        target = 0
        for size, index in zip(sizes, partner(*place)):
            target = target * size + index
        pairs.append((source, target))
    return lax.ppermute(x, axes, pairs)


def sum_heads(low):
    flip = min(lax.axis_size("side") - 1, 1)
    total = low.astype(F32)
    for k in partners(lax.axis_size("head")):
        low = total.astype(BF)
        other = joint(low, ("side", "head"), lambda s, h: (s ^ flip, h ^ k))
        total = low.astype(F32) + other.astype(F32)
    return total


def gather_rows(packed):
    ep_count, side_count = lax.axis_size("ep"), lax.axis_size("side")
    if (ep_count, side_count) == (4, 2):
        far = joint(packed, ("ep", "side"), lambda e, s: (e ^ (2 + s), s))
        near = joint(packed, ("ep", "side"), lambda e, s: (e ^ 1, s ^ 1))
        return jnp.concatenate([packed, near, far, swap(far, "side", 1)], 0)
    for k in partners(ep_count):
        packed = jnp.concatenate([packed, swap(packed, "ep", k)], 0)
    return packed


def source_of(block):
    me = lax.axis_index("ep")
    if (lax.axis_size("ep"), lax.axis_size("side")) == (4, 2) and block >= 2:
        side = lax.axis_index("side")
        return me ^ (block + side if block == 2 else block - side)
    return me ^ block


def sum_over(low, axis):
    total = low.astype(F32)
    for k in partners(lax.axis_size(axis)):
        low = total.astype(BF)
        total = low.astype(F32) + swap(low, axis, k).astype(F32)
    return total


def attend_kernel(
    lengths_hbm,
    query_hbm,
    new_key_hbm,
    new_value_hbm,
    cache_keys_hbm,
    cache_values_hbm,
    expert_ids_hbm,
    route_weights_hbm,
    hidden_hbm,
    norm_gain_hbm,
    out_weight_hbm,
    partial_out,
    coefficient_out,
    norm_gain_out,
    lengths,
    query,
    new_key,
    new_value,
    cache_keys,
    cache_values,
    expert_ids,
    route_weights,
    hidden,
    out_weight,
    arrivals,
    weight_arrivals,
):
    moves = [
        (lengths_hbm, lengths),
        (query_hbm, query),
        (cache_keys_hbm, cache_keys),
        (new_key_hbm, new_key),
        (new_value_hbm, new_value),
        (cache_values_hbm, cache_values),
        (expert_ids_hbm, expert_ids),
        (route_weights_hbm, route_weights),
        (hidden_hbm, hidden),
        (norm_gain_hbm, norm_gain_out),
    ]
    copies = [
        pltpu.make_async_copy(source, target, arrivals.at[i])
        for i, (source, target) in enumerate(moves)
    ]
    rows, kv_local, width = query.shape
    depth = out_weight.shape[2]
    step = math.gcd(width, 2 * HD)
    pieces = [(g, c) for g in range(kv_local) for c in range(0, width, step)]
    weight_copies = [
        pltpu.make_async_copy(
            out_weight_hbm.at[g, pl.ds(c, step)],
            out_weight.at[g, pl.ds(c, step)],
            weight_arrivals.at[i],
        )
        for i, (g, c) in enumerate(pieces)
    ]
    for copy in copies + weight_copies:
        copy.start()
    context = cache_keys.shape[1]
    heads = width // HD
    total = rows * context
    scale = 1.0 / math.sqrt(HD)
    pairs = [(g, n) for g in range(kv_local) for n in range(heads)]
    for copy in copies[:4]:
        copy.wait()
    zero = jnp.zeros((rows, HD), BF)
    queries = [query[:, g, n * HD : (n + 1) * HD] for g, n in pairs]
    placed = [
        jnp.concatenate([q if g == other else zero for other in range(kv_local)], 1)
        for (g, n), q in zip(pairs, queries)
    ]
    stacked = jnp.concatenate(placed, 0)
    keys = cache_keys[...].reshape(total, kv_local * HD)
    contract = (((1,), (1,)), ((), ()))
    scores = lax.dot_general(stacked, keys, contract, preferred_element_type=F32) * scale
    scores = scores.reshape(len(pairs), rows, total)
    row = lax.broadcasted_iota(jnp.int32, (rows, total), 0)
    column = lax.broadcasted_iota(jnp.int32, (rows, total), 1)
    start = row * context
    end = start
    for r in range(rows):
        end = jnp.where(row == r, r * context + lengths[r], end)
    usable = (column >= start) & (column < end)
    scores = jnp.where(usable[None], scores, F32(-1e30))
    fresh = jnp.stack(
        [
            jnp.sum(
                q.astype(F32) * new_key[:, g * HD : (g + 1) * HD].astype(F32), 1, keepdims=True
            )
            for (g, n), q in zip(pairs, queries)
        ],
        0,
    ) * scale
    highest = jnp.maximum(jnp.max(scores, -1, keepdims=True), fresh)
    weights = jnp.exp(scores - highest)
    own = jnp.exp(fresh - highest)
    denominator = jnp.sum(weights, -1, keepdims=True) + own
    low = weights.astype(BF).reshape(len(pairs) * rows, total)
    for copy in copies[4:8]:
        copy.wait()
    values = cache_values[...].reshape(total, kv_local * HD)
    mixed = jnp.dot(low, values, preferred_element_type=F32)
    mixed = mixed.reshape(len(pairs), rows, kv_local * HD)
    own_low = own.astype(BF).astype(F32)
    attended = []
    for i, (g, n) in enumerate(pairs):
        block = slice(g * HD, (g + 1) * HD)
        value = mixed[i][:, block] + own_low[i] * new_value[:, block].astype(F32)
        attended.append((value / denominator[i]).astype(BF))
    attended = jnp.concatenate(attended, 1)
    experts = coefficient_out.shape[1] // 2
    weight = route_weights[...]
    share = weight / jnp.sum(weight, 1, keepdims=True)
    lane = lax.broadcasted_iota(jnp.int32, (rows, experts), 1)
    coefficient = jnp.zeros((rows, experts), F32)
    for k in range(weight.shape[1]):
        coefficient += jnp.where(lane == expert_ids[:, k : k + 1], share[:, k : k + 1], F32(0.0))
    high = coefficient.astype(BF)
    rest = (coefficient - high.astype(F32)).astype(BF)
    coefficient_out[...] = jnp.concatenate([high, rest], 1)
    for copy in copies[8:]:
        copy.wait()
    first = (lax.axis_index("side") == 0) & (lax.axis_index("head") == 0)
    projected = jnp.where(first, hidden[...].astype(F32), F32(0.0))
    for copy, (g, c) in zip(weight_copies, pieces):
        copy.wait()
        low = g * width + c
        projected += jnp.dot(
            attended[:, low : low + step], out_weight[g, c : c + step], preferred_element_type=F32
        )
    partial_out[...] = projected.astype(BF)


def add_kernel(mine, other, out):
    out[...] = (mine[...].astype(F32) + other[...].astype(F32)).astype(BF)


def take_kernel(stream, out):
    width = out.shape[1]
    me = lax.axis_index("head")
    taken = stream[:, :width]
    for h in range(1, stream.shape[1] // width):
        taken = jnp.where(me == h, stream[:, h * width : (h + 1) * width], taken)
    out[...] = taken


def expert_kernel(
    gathered, norm_gain, gate_weight, up_weight, down_weight, out, inner, width
):
    count, depth, hidden_units = gate_weight.shape
    experts = (gathered.shape[1] - depth) // 2
    rows = gathered.shape[0]
    stream = gathered[:, :depth].astype(F32)
    norm = lax.rsqrt(jnp.mean(stream * stream, -1, keepdims=True) + 1e-06)
    normed = (stream * norm * norm_gain[...]).astype(BF)
    coefficient = gathered[:, depth : depth + experts].astype(F32) + gathered[
        :, depth + experts :
    ].astype(F32)
    lane = lax.broadcasted_iota(jnp.int32, (rows, experts), 1)
    me = lax.axis_index("ep")
    first = (me * lax.axis_size("side") + lax.axis_index("side")) * count
    for e in range(count):
        gate = jnp.dot(normed, gate_weight[e], preferred_element_type=F32)
        upper = jnp.dot(normed, up_weight[e], preferred_element_type=F32)
        share = jnp.sum(jnp.where(lane == first + e, coefficient, F32(0.0)), 1, keepdims=True)
        value = gate / (1.0 + jnp.exp(-gate)) * upper * share
        inner[:, e * hidden_units : (e + 1) * hidden_units] = value.astype(BF)
    result = jnp.dot(
        inner[...],
        down_weight[...].reshape(count * hidden_units, depth),
        preferred_element_type=F32,
    ).astype(BF)
    blocks, block_rows, _ = out.shape
    heads = depth // width
    for j in range(blocks // heads):
        target = source_of(j)
        for h in range(heads):
            out[target * heads + h] = result[
                j * block_rows : (j + 1) * block_rows, h * width : (h + 1) * width
            ]


def run_experts(gathered, gain, gate_weight, up_weight, down_weight, head_count, ep_count):
    local_count, depth, hidden_units = gate_weight.shape
    rows = gathered.shape[0] // ep_count
    width = depth // head_count
    weight_bytes = 2 * (gate_weight.size + up_weight.size + down_weight.size)
    return pl.pallas_call(
        functools.partial(expert_kernel, width=width),
        out_shape=jax.ShapeDtypeStruct((ep_count * head_count, rows, width), BF),
        in_specs=[VMEM] * 5,
        out_specs=VMEM,
        scratch_shapes=[
            pltpu.VMEM((ep_count * rows, local_count * hidden_units), BF),
        ],
        compiler_params=pltpu.CompilerParams(vmem_limit_bytes=8 << 20),
        cost_estimate=pl.CostEstimate(
            flops=ep_count * rows * weight_bytes, bytes_accessed=weight_bytes, transcendentals=0
        ),
        name="experts",
    )(
        in_vmem(gathered),
        in_vmem(gain),
        in_vmem(gate_weight),
        in_vmem(up_weight),
        in_vmem(down_weight),
    )


def on_device(
    hidden,
    query,
    new_key,
    new_value,
    cache_keys,
    cache_values,
    lengths,
    out_weight,
    norm_gain,
    expert_ids,
    route_weights,
    gate_weight,
    up_weight,
    down_weight,
):
    ep_count = lax.axis_size("ep")
    side_count = lax.axis_size("side")
    head_count = lax.axis_size("head")
    rows, depth = hidden.shape
    local_count, _, hidden_units = gate_weight.shape
    experts = local_count * ep_count * side_count
    width = depth // head_count
    top = expert_ids.shape[1]
    gain = norm_gain.reshape(1, depth)
    pieces = out_weight.shape[0] * (out_weight.shape[1] // math.gcd(out_weight.shape[1], 2 * HD))
    partial_value, coefficient, gain_near = pl.pallas_call(
        attend_kernel,
        out_shape=(
            pltpu.VMEM((rows, depth), BF),
            pltpu.VMEM((rows, 2 * experts), BF),
            pltpu.VMEM(gain.shape, F32),
        ),
        in_specs=[HBM] * 11,
        out_specs=(VMEM,) * 3,
        scratch_shapes=[
            pltpu.SMEM(lengths.shape, jnp.int32),
            pltpu.VMEM(query.shape, BF),
            pltpu.VMEM(new_key.shape, BF),
            pltpu.VMEM(new_value.shape, BF),
            pltpu.VMEM(cache_keys.shape, BF),
            pltpu.VMEM(cache_values.shape, BF),
            pltpu.VMEM((rows, top), jnp.int32),
            pltpu.VMEM((rows, top), F32),
            pltpu.VMEM(hidden.shape, BF),
            pltpu.VMEM(out_weight.shape, BF),
            pltpu.SemaphoreType.DMA((10,)),
            pltpu.SemaphoreType.DMA((pieces,)),
        ],
        compiler_params=pltpu.CompilerParams(vmem_limit_bytes=16 << 20),
        cost_estimate=pl.CostEstimate(
            flops=10**12, bytes_accessed=200 * 10**6, transcendentals=0
        ),
        name="attend",
    )(
        in_hbm(lengths),
        in_hbm(query),
        in_hbm(new_key),
        in_hbm(new_value),
        in_hbm(cache_keys),
        in_hbm(cache_values),
        in_hbm(expert_ids),
        in_hbm(route_weights),
        in_hbm(hidden),
        in_hbm(gain),
        in_hbm(out_weight),
    )
    for k in partners(side_count):
        other = swap(partial_value, "side", k)
        partial_value = pl.pallas_call(
            add_kernel,
            out_shape=pltpu.VMEM((rows, depth), BF),
            in_specs=[VMEM] * 2,
            out_specs=VMEM,
            compiler_params=pltpu.CompilerParams(vmem_limit_bytes=4 << 20),
            name="side_sum",
        )(in_vmem(partial_value), in_vmem(other))
    stream = sum_heads(partial_value)
    after_attention = pl.pallas_call(
        take_kernel,
        out_shape=jax.ShapeDtypeStruct((rows, width), F32),
        in_specs=[VMEM],
        out_specs=VMEM,
        compiler_params=pltpu.CompilerParams(vmem_limit_bytes=4 << 20),
        cost_estimate=pl.CostEstimate(flops=10**4, bytes_accessed=10**5, transcendentals=0),
        name="take",
    )(in_vmem(stream))
    packed = jnp.concatenate([stream.astype(BF), coefficient], 1)
    gathered = gather_rows(packed)
    result = run_experts(
        gathered, gain_near, gate_weight, up_weight, down_weight, head_count, ep_count
    )
    arrived = lax.all_to_all(result, ("ep", "head"), 0, 0, tiled=True)
    local_sum = jnp.sum(arrived.astype(F32), 0).astype(BF)
    expert_sum = sum_over(local_sum, "side").astype(BF)
    return (after_attention, expert_sum)


def solution(mesh):
    placed = (
        P(("groups", "ep"), None),
        P(("groups", "ep"), "head", "side"),
        P(("groups", "ep"), "head"),
        P(("groups", "ep"), "head"),
        P(("groups", "ep"), None, "head"),
        P(("groups", "ep"), None, "head"),
        P(("groups", "ep")),
        P("head", "side", None),
        P(),
        P(("groups", "ep"), None),
        P(("groups", "ep"), None),
        P(("ep", "side"), None, "head"),
        P(("ep", "side"), None, "head"),
        P(("ep", "side"), "head", None),
    )
    return jax.shard_map(
        on_device,
        mesh=mesh,
        in_specs=placed,
        out_specs=(P(("groups", "ep"), "head"), P(("groups", "ep"), "head")),
        check_vma=False,
    )
```

```python
import functools
import math

import jax
import jax.numpy as jnp
from jax import lax
from jax.experimental import pallas as pl
from jax.experimental.pallas import tpu as pltpu
from jax.sharding import PartitionSpec as P

HD = 128
BF = jnp.bfloat16
F32 = jnp.float32
VMEM = pl.BlockSpec(memory_space=pltpu.VMEM)
HBM = pl.BlockSpec(memory_space=pltpu.HBM)


def in_vmem(x):
    return pltpu.with_memory_space_constraint(x, pltpu.VMEM)


def in_hbm(x):
    return pltpu.with_memory_space_constraint(x, pltpu.HBM)


def partners(count):
    steps = []
    k = 1
    while k < count:
        steps.append(k)
        k *= 2
    return steps


def swap(x, axis, k):
    count = lax.axis_size(axis)
    return lax.ppermute(x, axis, [(i, i ^ k) for i in range(count)])


def joint(x, axes, partner):
    sizes = [lax.axis_size(axis) for axis in axes]
    pairs = []
    for source in range(math.prod(sizes)):
        rest, place = source, []
        for size in reversed(sizes):
            place.insert(0, rest % size)
            rest //= size
        target = 0
        for size, index in zip(sizes, partner(*place)):
            target = target * size + index
        pairs.append((source, target))
    return lax.ppermute(x, axes, pairs)


def sum_heads(low):
    flip = min(lax.axis_size("side") - 1, 1)
    total = low.astype(F32)
    for k in partners(lax.axis_size("head")):
        low = total.astype(BF)
        other = joint(low, ("side", "head"), lambda s, h: (s ^ flip, h ^ k))
        total = low.astype(F32) + other.astype(F32)
    return total


def split_gather():
    sizes = [lax.axis_size(axis) for axis in ("ep", "side", "head")]
    return sizes == [4, 2, 2]


def gather_rows(packed):
    if split_gather():
        axes = ("ep", "side", "head")
        second = joint(packed, axes, lambda e, s, h: (e ^ (1 + s), s, h))
        first = joint(packed, axes, lambda e, s, h: (e ^ 3 * s, s, h ^ 1 - s))
        held = jnp.concatenate([second, first], 0)
        return [packed, held, swap(held, "side", 1)]
    for k in partners(lax.axis_size("ep")):
        packed = jnp.concatenate([packed, swap(packed, "ep", k)], 0)
    return [packed]


def in_order(pieces):
    if len(pieces) == 1:
        return pieces[0][...]
    own, held, swapped = [piece[...] for piece in pieces]
    rows = own.shape[0]
    odd = lax.axis_index("side") == 1
    near = jnp.where(odd, swapped[:rows], held[:rows])
    far = jnp.where(odd, held, swapped)
    return jnp.concatenate([own, near, far], 0)


def sum_over(low, axis):
    total = low.astype(F32)
    for k in partners(lax.axis_size(axis)):
        low = total.astype(BF)
        total = low.astype(F32) + swap(low, axis, k).astype(F32)
    return total


def attend_kernel(
    lengths_hbm,
    query_hbm,
    new_key_hbm,
    new_value_hbm,
    cache_keys_hbm,
    cache_values_hbm,
    expert_ids_hbm,
    route_weights_hbm,
    hidden_hbm,
    norm_gain_hbm,
    out_weight_hbm,
    partial_out,
    coefficient_out,
    norm_gain_out,
    lengths,
    query,
    new_key,
    new_value,
    cache_keys,
    cache_values,
    expert_ids,
    route_weights,
    hidden,
    out_weight,
    arrivals,
    weight_arrivals,
):
    moves = [
        (lengths_hbm, lengths),
        (query_hbm, query),
        (cache_keys_hbm, cache_keys),
        (new_key_hbm, new_key),
        (new_value_hbm, new_value),
        (cache_values_hbm, cache_values),
        (expert_ids_hbm, expert_ids),
        (route_weights_hbm, route_weights),
        (hidden_hbm, hidden),
        (norm_gain_hbm, norm_gain_out),
    ]
    copies = [
        pltpu.make_async_copy(source, target, arrivals.at[i])
        for i, (source, target) in enumerate(moves)
    ]
    rows, kv_local, width = query.shape
    depth = out_weight.shape[2]
    step = math.gcd(width, 2 * HD)
    pieces = [(g, c) for g in range(kv_local) for c in range(0, width, step)]
    weight_copies = [
        pltpu.make_async_copy(
            out_weight_hbm.at[g, pl.ds(c, step)],
            out_weight.at[g, pl.ds(c, step)],
            weight_arrivals.at[i],
        )
        for i, (g, c) in enumerate(pieces)
    ]
    for copy in copies + weight_copies:
        copy.start()
    context = cache_keys.shape[1]
    heads = width // HD
    total = rows * context
    scale = 1.0 / math.sqrt(HD)
    pairs = [(g, n) for g in range(kv_local) for n in range(heads)]
    for copy in copies[:4]:
        copy.wait()
    zero = jnp.zeros((rows, HD), BF)
    queries = [query[:, g, n * HD : (n + 1) * HD] for g, n in pairs]
    placed = [
        jnp.concatenate([q if g == other else zero for other in range(kv_local)], 1)
        for (g, n), q in zip(pairs, queries)
    ]
    stacked = jnp.concatenate(placed, 0)
    keys = cache_keys[...].reshape(total, kv_local * HD)
    contract = (((1,), (1,)), ((), ()))
    scores = lax.dot_general(stacked, keys, contract, preferred_element_type=F32) * scale
    scores = scores.reshape(len(pairs), rows, total)
    row = lax.broadcasted_iota(jnp.int32, (rows, total), 0)
    column = lax.broadcasted_iota(jnp.int32, (rows, total), 1)
    start = row * context
    end = start
    for r in range(rows):
        end = jnp.where(row == r, r * context + lengths[r], end)
    usable = (column >= start) & (column < end)
    scores = jnp.where(usable[None], scores, F32(-1e30))
    fresh = jnp.stack(
        [
            jnp.sum(
                q.astype(F32) * new_key[:, g * HD : (g + 1) * HD].astype(F32), 1, keepdims=True
            )
            for (g, n), q in zip(pairs, queries)
        ],
        0,
    ) * scale
    highest = jnp.maximum(jnp.max(scores, -1, keepdims=True), fresh)
    weights = jnp.exp(scores - highest)
    own = jnp.exp(fresh - highest)
    denominator = jnp.sum(weights, -1, keepdims=True) + own
    low = weights.astype(BF).reshape(len(pairs) * rows, total)
    for copy in copies[4:8]:
        copy.wait()
    values = cache_values[...].reshape(total, kv_local * HD)
    mixed = jnp.dot(low, values, preferred_element_type=F32)
    mixed = mixed.reshape(len(pairs), rows, kv_local * HD)
    own_low = own.astype(BF).astype(F32)
    attended = []
    for i, (g, n) in enumerate(pairs):
        block = slice(g * HD, (g + 1) * HD)
        value = mixed[i][:, block] + own_low[i] * new_value[:, block].astype(F32)
        attended.append((value / denominator[i]).astype(BF))
    attended = jnp.concatenate(attended, 1)
    experts = coefficient_out.shape[1] // 2
    weight = route_weights[...]
    share = weight / jnp.sum(weight, 1, keepdims=True)
    lane = lax.broadcasted_iota(jnp.int32, (rows, experts), 1)
    coefficient = jnp.zeros((rows, experts), F32)
    for k in range(weight.shape[1]):
        coefficient += jnp.where(lane == expert_ids[:, k : k + 1], share[:, k : k + 1], F32(0.0))
    high = coefficient.astype(BF)
    rest = (coefficient - high.astype(F32)).astype(BF)
    coefficient_out[...] = jnp.concatenate([high, rest], 1)
    for copy in copies[8:]:
        copy.wait()
    first = (lax.axis_index("side") == 0) & (lax.axis_index("head") == 0)
    projected = jnp.where(first, hidden[...].astype(F32), F32(0.0))
    for copy, (g, c) in zip(weight_copies, pieces):
        copy.wait()
        low = g * width + c
        projected += jnp.dot(
            attended[:, low : low + step], out_weight[g, c : c + step], preferred_element_type=F32
        )
    partial_out[...] = projected.astype(BF)


def add_kernel(mine, other, out):
    out[...] = (mine[...].astype(F32) + other[...].astype(F32)).astype(BF)


def take_kernel(stream, out):
    width = out.shape[1]
    me = lax.axis_index("head")
    taken = stream[:, :width]
    for h in range(1, stream.shape[1] // width):
        taken = jnp.where(me == h, stream[:, h * width : (h + 1) * width], taken)
    out[...] = taken


def expert_kernel(*refs, width, pieces):
    gathered = in_order(refs[:pieces])
    expert_body(gathered, *refs[pieces:], width)


def expert_body(
    gathered, norm_gain, gate_weight, up_weight, down_weight, out, inner, width
):
    count, depth, hidden_units = gate_weight.shape
    experts = (gathered.shape[1] - depth) // 2
    rows = gathered.shape[0]
    stream = gathered[:, :depth].astype(F32)
    norm = lax.rsqrt(jnp.mean(stream * stream, -1, keepdims=True) + 1e-06)
    normed = (stream * norm * norm_gain[...]).astype(BF)
    coefficient = gathered[:, depth : depth + experts].astype(F32) + gathered[
        :, depth + experts :
    ].astype(F32)
    lane = lax.broadcasted_iota(jnp.int32, (rows, experts), 1)
    me = lax.axis_index("ep")
    first = (me * lax.axis_size("side") + lax.axis_index("side")) * count
    for e in range(count):
        gate = jnp.dot(normed, gate_weight[e], preferred_element_type=F32)
        upper = jnp.dot(normed, up_weight[e], preferred_element_type=F32)
        share = jnp.sum(jnp.where(lane == first + e, coefficient, F32(0.0)), 1, keepdims=True)
        value = gate / (1.0 + jnp.exp(-gate)) * upper * share
        inner[:, e * hidden_units : (e + 1) * hidden_units] = value.astype(BF)
    result = jnp.dot(
        inner[...],
        down_weight[...].reshape(count * hidden_units, depth),
        preferred_element_type=F32,
    ).astype(BF)
    blocks, block_rows, _ = out.shape
    heads = depth // width
    for j in range(blocks // heads):
        target = me ^ j
        for h in range(heads):
            out[target * heads + h] = result[
                j * block_rows : (j + 1) * block_rows, h * width : (h + 1) * width
            ]


def run_experts(gathered, gain, gate_weight, up_weight, down_weight, head_count, ep_count):
    local_count, depth, hidden_units = gate_weight.shape
    rows = gathered[0].shape[0] if len(gathered) > 1 else gathered[0].shape[0] // ep_count
    width = depth // head_count
    weight_bytes = 2 * (gate_weight.size + up_weight.size + down_weight.size)
    return pl.pallas_call(
        functools.partial(expert_kernel, width=width, pieces=len(gathered)),
        out_shape=jax.ShapeDtypeStruct((ep_count * head_count, rows, width), BF),
        in_specs=[VMEM] * (4 + len(gathered)),
        out_specs=VMEM,
        scratch_shapes=[
            pltpu.VMEM((ep_count * rows, local_count * hidden_units), BF),
        ],
        compiler_params=pltpu.CompilerParams(vmem_limit_bytes=8 << 20),
        cost_estimate=pl.CostEstimate(
            flops=ep_count * rows * weight_bytes, bytes_accessed=weight_bytes, transcendentals=0
        ),
        name="experts",
    )(
        *[in_vmem(piece) for piece in gathered],
        in_vmem(gain),
        in_vmem(gate_weight),
        in_vmem(up_weight),
        in_vmem(down_weight),
    )


def on_device(
    hidden,
    query,
    new_key,
    new_value,
    cache_keys,
    cache_values,
    lengths,
    out_weight,
    norm_gain,
    expert_ids,
    route_weights,
    gate_weight,
    up_weight,
    down_weight,
):
    ep_count = lax.axis_size("ep")
    side_count = lax.axis_size("side")
    head_count = lax.axis_size("head")
    rows, depth = hidden.shape
    local_count, _, hidden_units = gate_weight.shape
    experts = local_count * ep_count * side_count
    width = depth // head_count
    top = expert_ids.shape[1]
    gain = norm_gain.reshape(1, depth)
    pieces = out_weight.shape[0] * (out_weight.shape[1] // math.gcd(out_weight.shape[1], 2 * HD))
    partial_value, coefficient, gain_near = pl.pallas_call(
        attend_kernel,
        out_shape=(
            pltpu.VMEM((rows, depth), BF),
            pltpu.VMEM((rows, 2 * experts), BF),
            pltpu.VMEM(gain.shape, F32),
        ),
        in_specs=[HBM] * 11,
        out_specs=(VMEM,) * 3,
        scratch_shapes=[
            pltpu.SMEM(lengths.shape, jnp.int32),
            pltpu.VMEM(query.shape, BF),
            pltpu.VMEM(new_key.shape, BF),
            pltpu.VMEM(new_value.shape, BF),
            pltpu.VMEM(cache_keys.shape, BF),
            pltpu.VMEM(cache_values.shape, BF),
            pltpu.VMEM((rows, top), jnp.int32),
            pltpu.VMEM((rows, top), F32),
            pltpu.VMEM(hidden.shape, BF),
            pltpu.VMEM(out_weight.shape, BF),
            pltpu.SemaphoreType.DMA((10,)),
            pltpu.SemaphoreType.DMA((pieces,)),
        ],
        compiler_params=pltpu.CompilerParams(vmem_limit_bytes=16 << 20),
        cost_estimate=pl.CostEstimate(
            flops=10**12, bytes_accessed=200 * 10**6, transcendentals=0
        ),
        name="attend",
    )(
        in_hbm(lengths),
        in_hbm(query),
        in_hbm(new_key),
        in_hbm(new_value),
        in_hbm(cache_keys),
        in_hbm(cache_values),
        in_hbm(expert_ids),
        in_hbm(route_weights),
        in_hbm(hidden),
        in_hbm(gain),
        in_hbm(out_weight),
    )
    for k in partners(side_count):
        other = swap(partial_value, "side", k)
        partial_value = pl.pallas_call(
            add_kernel,
            out_shape=pltpu.VMEM((rows, depth), BF),
            in_specs=[VMEM] * 2,
            out_specs=VMEM,
            compiler_params=pltpu.CompilerParams(vmem_limit_bytes=4 << 20),
            name="side_sum",
        )(in_vmem(partial_value), in_vmem(other))
    stream = sum_heads(partial_value)
    after_attention = pl.pallas_call(
        take_kernel,
        out_shape=jax.ShapeDtypeStruct((rows, width), F32),
        in_specs=[VMEM],
        out_specs=VMEM,
        compiler_params=pltpu.CompilerParams(vmem_limit_bytes=4 << 20),
        cost_estimate=pl.CostEstimate(flops=10**4, bytes_accessed=10**5, transcendentals=0),
        name="take",
    )(in_vmem(stream))
    packed = jnp.concatenate([stream.astype(BF), coefficient], 1)
    gathered = gather_rows(packed)
    result = run_experts(
        gathered, gain_near, gate_weight, up_weight, down_weight, head_count, ep_count
    )
    arrived = lax.all_to_all(result, ("ep", "head"), 0, 0, tiled=True)
    local_sum = jnp.sum(arrived.astype(F32), 0).astype(BF)
    expert_sum = sum_over(local_sum, "side").astype(BF)
    return (after_attention, expert_sum)


def solution(mesh):
    placed = (
        P(("groups", "ep"), None),
        P(("groups", "ep"), "head", "side"),
        P(("groups", "ep"), "head"),
        P(("groups", "ep"), "head"),
        P(("groups", "ep"), None, "head"),
        P(("groups", "ep"), None, "head"),
        P(("groups", "ep")),
        P("head", "side", None),
        P(),
        P(("groups", "ep"), None),
        P(("groups", "ep"), None),
        P(("ep", "side"), None, "head"),
        P(("ep", "side"), None, "head"),
        P(("ep", "side"), "head", None),
    )
    return jax.shard_map(
        on_device,
        mesh=mesh,
        in_specs=placed,
        out_specs=(P(("groups", "ep"), "head"), P(("groups", "ep"), "head")),
        check_vma=False,
    )
```

```python
import functools
import math

import jax
import jax.numpy as jnp
from jax import lax
from jax.experimental import pallas as pl
from jax.experimental.pallas import tpu as pltpu
from jax.sharding import PartitionSpec as P

HD = 128
BF = jnp.bfloat16
F32 = jnp.float32
VMEM = pl.BlockSpec(memory_space=pltpu.VMEM)
HBM = pl.BlockSpec(memory_space=pltpu.HBM)


def in_vmem(x):
    return pltpu.with_memory_space_constraint(x, pltpu.VMEM)


def in_hbm(x):
    return pltpu.with_memory_space_constraint(x, pltpu.HBM)


def partners(count):
    steps = []
    k = 1
    while k < count:
        steps.append(k)
        k *= 2
    return steps


def swap(x, axis, k):
    count = lax.axis_size(axis)
    return lax.ppermute(x, axis, [(i, i ^ k) for i in range(count)])


def joint(x, axes, partner):
    sizes = [lax.axis_size(axis) for axis in axes]
    pairs = []
    for source in range(math.prod(sizes)):
        rest, place = source, []
        for size in reversed(sizes):
            place.insert(0, rest % size)
            rest //= size
        target = 0
        for size, index in zip(sizes, partner(*place)):
            target = target * size + index
        pairs.append((source, target))
    return lax.ppermute(x, axes, pairs)


def sum_heads(low):
    flip = min(lax.axis_size("side") - 1, 1)
    total = low.astype(F32)
    for k in partners(lax.axis_size("head")):
        low = total.astype(BF)
        other = joint(low, ("side", "head"), lambda s, h: (s ^ flip, h ^ k))
        total = low.astype(F32) + other.astype(F32)
    return total


def split_gather():
    sizes = [lax.axis_size(axis) for axis in ("ep", "side", "head")]
    return sizes == [4, 2, 2]


def gather_rows(packed):
    if split_gather():
        axes = ("ep", "side", "head")
        second = joint(packed, axes, lambda e, s, h: (e ^ (1 + s), s, h))
        first = joint(packed, axes, lambda e, s, h: (e ^ 3 * s, s, h ^ 1 - s))
        held = jnp.concatenate([second, first], 0)
        return [packed, held, swap(held, "side", 1)]
    for k in partners(lax.axis_size("ep")):
        packed = jnp.concatenate([packed, swap(packed, "ep", k)], 0)
    return [packed]


def return_rows(give, keep):
    chip = (keep.astype(F32) + swap(give, "side", 1).astype(F32)).astype(BF)
    rows, width = chip.shape[0] // 2, chip.shape[1] // 2
    axes = ("ep", "side", "head")
    second = joint(chip[:rows], axes, lambda e, s, h: (e ^ (1 + s), s, h))
    first = joint(chip[rows:], axes, lambda e, s, h: (e ^ 3 * s, s, h ^ 1 - s))
    rest = jnp.where(lax.axis_index("side") == 1, first, chip[rows:])
    total = second.astype(F32) + rest.astype(F32)
    left = lax.axis_index("head") == 0
    mine = jnp.where(left, total[:, :width], total[:, width:])
    other = jnp.where(left, total[:, width:], total[:, :width]).astype(BF)
    arrived = joint(other, ("side", "head"), lambda s, h: (s ^ 1, h ^ 1))
    return (mine + arrived.astype(F32)).astype(BF)


def in_order(pieces):
    if len(pieces) == 1:
        return pieces[0][...]
    own, held, swapped = [piece[...] for piece in pieces]
    rows = own.shape[0]
    odd = lax.axis_index("side") == 1
    near = jnp.where(odd, swapped[:rows], held[:rows])
    far = jnp.where(odd, held, swapped)
    return jnp.concatenate([own, near, far], 0)


def sum_over(low, axis):
    total = low.astype(F32)
    for k in partners(lax.axis_size(axis)):
        low = total.astype(BF)
        total = low.astype(F32) + swap(low, axis, k).astype(F32)
    return total


def attend_kernel(
    lengths_hbm,
    query_hbm,
    new_key_hbm,
    new_value_hbm,
    cache_keys_hbm,
    cache_values_hbm,
    expert_ids_hbm,
    route_weights_hbm,
    hidden_hbm,
    norm_gain_hbm,
    out_weight_hbm,
    partial_out,
    coefficient_out,
    norm_gain_out,
    lengths,
    query,
    new_key,
    new_value,
    cache_keys,
    cache_values,
    expert_ids,
    route_weights,
    hidden,
    out_weight,
    arrivals,
    weight_arrivals,
):
    moves = [
        (lengths_hbm, lengths),
        (query_hbm, query),
        (cache_keys_hbm, cache_keys),
        (new_key_hbm, new_key),
        (new_value_hbm, new_value),
        (cache_values_hbm, cache_values),
        (expert_ids_hbm, expert_ids),
        (route_weights_hbm, route_weights),
        (hidden_hbm, hidden),
        (norm_gain_hbm, norm_gain_out),
    ]
    copies = [
        pltpu.make_async_copy(source, target, arrivals.at[i])
        for i, (source, target) in enumerate(moves)
    ]
    rows, kv_local, width = query.shape
    depth = out_weight.shape[2]
    step = math.gcd(width, 2 * HD)
    pieces = [(g, c) for g in range(kv_local) for c in range(0, width, step)]
    weight_copies = [
        pltpu.make_async_copy(
            out_weight_hbm.at[g, pl.ds(c, step)],
            out_weight.at[g, pl.ds(c, step)],
            weight_arrivals.at[i],
        )
        for i, (g, c) in enumerate(pieces)
    ]
    for copy in copies + weight_copies:
        copy.start()
    context = cache_keys.shape[1]
    heads = width // HD
    total = rows * context
    scale = 1.0 / math.sqrt(HD)
    pairs = [(g, n) for g in range(kv_local) for n in range(heads)]
    for copy in copies[:4]:
        copy.wait()
    zero = jnp.zeros((rows, HD), BF)
    queries = [query[:, g, n * HD : (n + 1) * HD] for g, n in pairs]
    placed = [
        jnp.concatenate([q if g == other else zero for other in range(kv_local)], 1)
        for (g, n), q in zip(pairs, queries)
    ]
    stacked = jnp.concatenate(placed, 0)
    keys = cache_keys[...].reshape(total, kv_local * HD)
    contract = (((1,), (1,)), ((), ()))
    scores = lax.dot_general(stacked, keys, contract, preferred_element_type=F32) * scale
    scores = scores.reshape(len(pairs), rows, total)
    row = lax.broadcasted_iota(jnp.int32, (rows, total), 0)
    column = lax.broadcasted_iota(jnp.int32, (rows, total), 1)
    start = row * context
    end = start
    for r in range(rows):
        end = jnp.where(row == r, r * context + lengths[r], end)
    usable = (column >= start) & (column < end)
    scores = jnp.where(usable[None], scores, F32(-1e30))
    fresh = jnp.stack(
        [
            jnp.sum(
                q.astype(F32) * new_key[:, g * HD : (g + 1) * HD].astype(F32), 1, keepdims=True
            )
            for (g, n), q in zip(pairs, queries)
        ],
        0,
    ) * scale
    highest = jnp.maximum(jnp.max(scores, -1, keepdims=True), fresh)
    weights = jnp.exp(scores - highest)
    own = jnp.exp(fresh - highest)
    denominator = jnp.sum(weights, -1, keepdims=True) + own
    low = weights.astype(BF).reshape(len(pairs) * rows, total)
    for copy in copies[4:8]:
        copy.wait()
    values = cache_values[...].reshape(total, kv_local * HD)
    mixed = jnp.dot(low, values, preferred_element_type=F32)
    mixed = mixed.reshape(len(pairs), rows, kv_local * HD)
    own_low = own.astype(BF).astype(F32)
    attended = []
    for i, (g, n) in enumerate(pairs):
        block = slice(g * HD, (g + 1) * HD)
        value = mixed[i][:, block] + own_low[i] * new_value[:, block].astype(F32)
        attended.append((value / denominator[i]).astype(BF))
    attended = jnp.concatenate(attended, 1)
    experts = coefficient_out.shape[1] // 2
    weight = route_weights[...]
    share = weight / jnp.sum(weight, 1, keepdims=True)
    lane = lax.broadcasted_iota(jnp.int32, (rows, experts), 1)
    coefficient = jnp.zeros((rows, experts), F32)
    for k in range(weight.shape[1]):
        coefficient += jnp.where(lane == expert_ids[:, k : k + 1], share[:, k : k + 1], F32(0.0))
    high = coefficient.astype(BF)
    rest = (coefficient - high.astype(F32)).astype(BF)
    coefficient_out[...] = jnp.concatenate([high, rest], 1)
    for copy in copies[8:]:
        copy.wait()
    first = (lax.axis_index("side") == 0) & (lax.axis_index("head") == 0)
    projected = jnp.where(first, hidden[...].astype(F32), F32(0.0))
    for copy, (g, c) in zip(weight_copies, pieces):
        copy.wait()
        low = g * width + c
        projected += jnp.dot(
            attended[:, low : low + step], out_weight[g, c : c + step], preferred_element_type=F32
        )
    partial_out[...] = projected.astype(BF)


def add_kernel(mine, other, out):
    out[...] = (mine[...].astype(F32) + other[...].astype(F32)).astype(BF)


def take_kernel(stream, out):
    width = out.shape[1]
    me = lax.axis_index("head")
    taken = stream[:, :width]
    for h in range(1, stream.shape[1] // width):
        taken = jnp.where(me == h, stream[:, h * width : (h + 1) * width], taken)
    out[...] = taken


def expert_kernel(*refs, width, pieces):
    gathered = in_order(refs[:pieces])
    expert_body(gathered, *refs[pieces:], width, pieces > 1)


def expert_body(gathered, norm_gain, gate_weight, up_weight, down_weight, *rest):
    *outs, inner, width, split = rest
    count, depth, hidden_units = gate_weight.shape
    experts = (gathered.shape[1] - depth) // 2
    rows = gathered.shape[0]
    stream = gathered[:, :depth].astype(F32)
    norm = lax.rsqrt(jnp.mean(stream * stream, -1, keepdims=True) + 1e-06)
    normed = (stream * norm * norm_gain[...]).astype(BF)
    coefficient = gathered[:, depth : depth + experts].astype(F32) + gathered[
        :, depth + experts :
    ].astype(F32)
    lane = lax.broadcasted_iota(jnp.int32, (rows, experts), 1)
    me = lax.axis_index("ep")
    first = (me * lax.axis_size("side") + lax.axis_index("side")) * count
    for e in range(count):
        gate = jnp.dot(normed, gate_weight[e], preferred_element_type=F32)
        upper = jnp.dot(normed, up_weight[e], preferred_element_type=F32)
        share = jnp.sum(jnp.where(lane == first + e, coefficient, F32(0.0)), 1, keepdims=True)
        value = gate / (1.0 + jnp.exp(-gate)) * upper * share
        inner[:, e * hidden_units : (e + 1) * hidden_units] = value.astype(BF)
    result = jnp.dot(
        inner[...],
        down_weight[...].reshape(count * hidden_units, depth),
        preferred_element_type=F32,
    ).astype(BF)
    if split:
        pair = rows // 2
        block = pair // 2
        close = jnp.concatenate([result[block:pair], result[:block]], 0)
        odd = lax.axis_index("side") == 1
        outs[0][...] = jnp.where(odd, close, result[pair:])
        outs[1][...] = jnp.where(odd, result[pair:], close)
        return
    out = outs[0]
    blocks, block_rows, _ = out.shape
    heads = depth // width
    for j in range(blocks // heads):
        target = me ^ j
        for h in range(heads):
            out[target * heads + h] = result[
                j * block_rows : (j + 1) * block_rows, h * width : (h + 1) * width
            ]


def run_experts(gathered, gain, gate_weight, up_weight, down_weight, head_count, ep_count):
    local_count, depth, hidden_units = gate_weight.shape
    rows = gathered[0].shape[0] if len(gathered) > 1 else gathered[0].shape[0] // ep_count
    width = depth // head_count
    if len(gathered) > 1:
        out_shape = [jax.ShapeDtypeStruct((ep_count * rows // 2, depth), BF)] * 2
    else:
        out_shape = [jax.ShapeDtypeStruct((ep_count * head_count, rows, width), BF)]
    weight_bytes = 2 * (gate_weight.size + up_weight.size + down_weight.size)
    return pl.pallas_call(
        functools.partial(expert_kernel, width=width, pieces=len(gathered)),
        out_shape=out_shape,
        in_specs=[VMEM] * (4 + len(gathered)),
        out_specs=[VMEM] * len(out_shape),
        scratch_shapes=[
            pltpu.VMEM((ep_count * rows, local_count * hidden_units), BF),
        ],
        compiler_params=pltpu.CompilerParams(vmem_limit_bytes=8 << 20),
        cost_estimate=pl.CostEstimate(
            flops=ep_count * rows * weight_bytes, bytes_accessed=weight_bytes, transcendentals=0
        ),
        name="experts",
    )(
        *[in_vmem(piece) for piece in gathered],
        in_vmem(gain),
        in_vmem(gate_weight),
        in_vmem(up_weight),
        in_vmem(down_weight),
    )


def on_device(
    hidden,
    query,
    new_key,
    new_value,
    cache_keys,
    cache_values,
    lengths,
    out_weight,
    norm_gain,
    expert_ids,
    route_weights,
    gate_weight,
    up_weight,
    down_weight,
):
    ep_count = lax.axis_size("ep")
    side_count = lax.axis_size("side")
    head_count = lax.axis_size("head")
    rows, depth = hidden.shape
    local_count, _, hidden_units = gate_weight.shape
    experts = local_count * ep_count * side_count
    width = depth // head_count
    top = expert_ids.shape[1]
    gain = norm_gain.reshape(1, depth)
    pieces = out_weight.shape[0] * (out_weight.shape[1] // math.gcd(out_weight.shape[1], 2 * HD))
    partial_value, coefficient, gain_near = pl.pallas_call(
        attend_kernel,
        out_shape=(
            pltpu.VMEM((rows, depth), BF),
            pltpu.VMEM((rows, 2 * experts), BF),
            pltpu.VMEM(gain.shape, F32),
        ),
        in_specs=[HBM] * 11,
        out_specs=(VMEM,) * 3,
        scratch_shapes=[
            pltpu.SMEM(lengths.shape, jnp.int32),
            pltpu.VMEM(query.shape, BF),
            pltpu.VMEM(new_key.shape, BF),
            pltpu.VMEM(new_value.shape, BF),
            pltpu.VMEM(cache_keys.shape, BF),
            pltpu.VMEM(cache_values.shape, BF),
            pltpu.VMEM((rows, top), jnp.int32),
            pltpu.VMEM((rows, top), F32),
            pltpu.VMEM(hidden.shape, BF),
            pltpu.VMEM(out_weight.shape, BF),
            pltpu.SemaphoreType.DMA((10,)),
            pltpu.SemaphoreType.DMA((pieces,)),
        ],
        compiler_params=pltpu.CompilerParams(vmem_limit_bytes=16 << 20),
        cost_estimate=pl.CostEstimate(
            flops=10**12, bytes_accessed=200 * 10**6, transcendentals=0
        ),
        name="attend",
    )(
        in_hbm(lengths),
        in_hbm(query),
        in_hbm(new_key),
        in_hbm(new_value),
        in_hbm(cache_keys),
        in_hbm(cache_values),
        in_hbm(expert_ids),
        in_hbm(route_weights),
        in_hbm(hidden),
        in_hbm(gain),
        in_hbm(out_weight),
    )
    for k in partners(side_count):
        other = swap(partial_value, "side", k)
        partial_value = pl.pallas_call(
            add_kernel,
            out_shape=pltpu.VMEM((rows, depth), BF),
            in_specs=[VMEM] * 2,
            out_specs=VMEM,
            compiler_params=pltpu.CompilerParams(vmem_limit_bytes=4 << 20),
            name="side_sum",
        )(in_vmem(partial_value), in_vmem(other))
    stream = sum_heads(partial_value)
    after_attention = pl.pallas_call(
        take_kernel,
        out_shape=jax.ShapeDtypeStruct((rows, width), F32),
        in_specs=[VMEM],
        out_specs=VMEM,
        compiler_params=pltpu.CompilerParams(vmem_limit_bytes=4 << 20),
        cost_estimate=pl.CostEstimate(flops=10**4, bytes_accessed=10**5, transcendentals=0),
        name="take",
    )(in_vmem(stream))
    packed = jnp.concatenate([stream.astype(BF), coefficient], 1)
    gathered = gather_rows(packed)
    result = run_experts(
        gathered, gain_near, gate_weight, up_weight, down_weight, head_count, ep_count
    )
    if len(result) > 1:
        local_sum = return_rows(*result)
    else:
        arrived = lax.all_to_all(result[0], ("ep", "head"), 0, 0, tiled=True)
        local_sum = jnp.sum(arrived.astype(F32), 0).astype(BF)
    expert_sum = sum_over(local_sum, "side").astype(BF)
    return (after_attention, expert_sum)


def solution(mesh):
    placed = (
        P(("groups", "ep"), None),
        P(("groups", "ep"), "head", "side"),
        P(("groups", "ep"), "head"),
        P(("groups", "ep"), "head"),
        P(("groups", "ep"), None, "head"),
        P(("groups", "ep"), None, "head"),
        P(("groups", "ep")),
        P("head", "side", None),
        P(),
        P(("groups", "ep"), None),
        P(("groups", "ep"), None),
        P(("ep", "side"), None, "head"),
        P(("ep", "side"), None, "head"),
        P(("ep", "side"), "head", None),
    )
    return jax.shard_map(
        on_device,
        mesh=mesh,
        in_specs=placed,
        out_specs=(P(("groups", "ep"), "head"), P(("groups", "ep"), "head")),
        check_vma=False,
    )
```

```python
import functools
import math

import jax
import jax.numpy as jnp
from jax import lax
from jax.experimental import pallas as pl
from jax.experimental.pallas import tpu as pltpu
from jax.sharding import PartitionSpec as P

HD = 128
BF = jnp.bfloat16
F32 = jnp.float32
VMEM = pl.BlockSpec(memory_space=pltpu.VMEM)
HBM = pl.BlockSpec(memory_space=pltpu.HBM)


def in_vmem(x):
    return pltpu.with_memory_space_constraint(x, pltpu.VMEM)


def in_hbm(x):
    return pltpu.with_memory_space_constraint(x, pltpu.HBM)


def partners(count):
    steps = []
    k = 1
    while k < count:
        steps.append(k)
        k *= 2
    return steps


def swap(x, axis, k):
    count = lax.axis_size(axis)
    return lax.ppermute(x, axis, [(i, i ^ k) for i in range(count)])


def joint(x, axes, partner):
    sizes = [lax.axis_size(axis) for axis in axes]
    pairs = []
    for source in range(math.prod(sizes)):
        rest, place = source, []
        for size in reversed(sizes):
            place.insert(0, rest % size)
            rest //= size
        target = 0
        for size, index in zip(sizes, partner(*place)):
            target = target * size + index
        pairs.append((source, target))
    return lax.ppermute(x, axes, pairs)


def sum_heads(low):
    flip = min(lax.axis_size("side") - 1, 1)
    total = low.astype(F32)
    for k in partners(lax.axis_size("head")):
        low = total.astype(BF)
        other = joint(low, ("side", "head"), lambda s, h: (s ^ flip, h ^ k))
        total = low.astype(F32) + other.astype(F32)
    return total


def split_gather():
    sizes = [lax.axis_size(axis) for axis in ("ep", "side", "head")]
    return sizes == [4, 2, 2]


def gather_rows(packed):
    if split_gather():
        axes = ("ep", "side", "head")
        second = joint(packed, axes, lambda e, s, h: (e ^ (1 + s), s, h))
        first = joint(packed, axes, lambda e, s, h: (e ^ 3 * s, s, h ^ 1 - s))
        held = jnp.concatenate([second, first], 0)
        return [packed, jnp.concatenate([held, swap(held, "side", 1)], 0)]
    for k in partners(lax.axis_size("ep")):
        packed = jnp.concatenate([packed, swap(packed, "ep", k)], 0)
    return [packed]


def return_rows(give, keep):
    chip = (keep.astype(F32) + swap(give, "side", 1).astype(F32)).astype(BF)
    rows, width = chip.shape[0] // 2, chip.shape[1] // 2
    axes = ("ep", "side", "head")
    second = joint(chip[:rows], axes, lambda e, s, h: (e ^ (1 + s), s, h))
    first = joint(chip[rows:], axes, lambda e, s, h: (e ^ 3 * s, s, h ^ 1 - s))
    rest = jnp.where(lax.axis_index("side") == 1, first, chip[rows:])
    total = second.astype(F32) + rest.astype(F32)
    left = lax.axis_index("head") == 0
    mine = jnp.where(left, total[:, :width], total[:, width:])
    other = jnp.where(left, total[:, width:], total[:, :width]).astype(BF)
    arrived = joint(other, ("side", "head"), lambda s, h: (s ^ 1, h ^ 1))
    return (mine + arrived.astype(F32)).astype(BF)


def in_order(pieces):
    if len(pieces) == 1:
        return pieces[0][...]
    own, both = pieces
    rows = own.shape[0]
    side = lax.axis_index("side")
    near = pl.multiple_of(side * 2 * rows, rows)
    far = pl.multiple_of((1 - side) * 2 * rows, rows)
    blocks = [own[...], both[pl.ds(near, rows)], both[pl.ds(far, 2 * rows)]]
    return jnp.concatenate(blocks, 0)


def sum_over(low, axis):
    total = low.astype(F32)
    for k in partners(lax.axis_size(axis)):
        low = total.astype(BF)
        total = low.astype(F32) + swap(low, axis, k).astype(F32)
    return total


def attend_kernel(
    lengths_hbm,
    query_hbm,
    new_key_hbm,
    new_value_hbm,
    cache_keys_hbm,
    cache_values_hbm,
    expert_ids_hbm,
    route_weights_hbm,
    hidden_hbm,
    norm_gain_hbm,
    out_weight_hbm,
    partial_out,
    coefficient_out,
    norm_gain_out,
    lengths,
    query,
    new_key,
    new_value,
    cache_keys,
    cache_values,
    expert_ids,
    route_weights,
    hidden,
    out_weight,
    arrivals,
    weight_arrivals,
):
    moves = [
        (lengths_hbm, lengths),
        (query_hbm, query),
        (cache_keys_hbm, cache_keys),
        (new_key_hbm, new_key),
        (new_value_hbm, new_value),
        (cache_values_hbm, cache_values),
        (expert_ids_hbm, expert_ids),
        (route_weights_hbm, route_weights),
        (hidden_hbm, hidden),
        (norm_gain_hbm, norm_gain_out),
    ]
    copies = [
        pltpu.make_async_copy(source, target, arrivals.at[i])
        for i, (source, target) in enumerate(moves)
    ]
    rows, kv_local, width = query.shape
    depth = out_weight.shape[2]
    step = math.gcd(width, 2 * HD)
    pieces = [(g, c) for g in range(kv_local) for c in range(0, width, step)]
    weight_copies = [
        pltpu.make_async_copy(
            out_weight_hbm.at[g, pl.ds(c, step)],
            out_weight.at[g, pl.ds(c, step)],
            weight_arrivals.at[i],
        )
        for i, (g, c) in enumerate(pieces)
    ]
    for copy in copies + weight_copies:
        copy.start()
    context = cache_keys.shape[1]
    heads = width // HD
    total = rows * context
    scale = 1.0 / math.sqrt(HD)
    pairs = [(g, n) for g in range(kv_local) for n in range(heads)]
    for copy in copies[:4]:
        copy.wait()
    zero = jnp.zeros((rows, HD), BF)
    queries = [query[:, g, n * HD : (n + 1) * HD] for g, n in pairs]
    placed = [
        jnp.concatenate([q if g == other else zero for other in range(kv_local)], 1)
        for (g, n), q in zip(pairs, queries)
    ]
    stacked = jnp.concatenate(placed, 0)
    keys = cache_keys[...].reshape(total, kv_local * HD)
    contract = (((1,), (1,)), ((), ()))
    scores = lax.dot_general(stacked, keys, contract, preferred_element_type=F32) * scale
    scores = scores.reshape(len(pairs), rows, total)
    row = lax.broadcasted_iota(jnp.int32, (rows, total), 0)
    column = lax.broadcasted_iota(jnp.int32, (rows, total), 1)
    start = row * context
    end = start
    for r in range(rows):
        end = jnp.where(row == r, r * context + lengths[r], end)
    usable = (column >= start) & (column < end)
    scores = jnp.where(usable[None], scores, F32(-1e30))
    fresh = jnp.stack(
        [
            jnp.sum(
                q.astype(F32) * new_key[:, g * HD : (g + 1) * HD].astype(F32), 1, keepdims=True
            )
            for (g, n), q in zip(pairs, queries)
        ],
        0,
    ) * scale
    highest = jnp.maximum(jnp.max(scores, -1, keepdims=True), fresh)
    weights = jnp.exp(scores - highest)
    own = jnp.exp(fresh - highest)
    denominator = jnp.sum(weights, -1, keepdims=True) + own
    low = weights.astype(BF).reshape(len(pairs) * rows, total)
    for copy in copies[4:8]:
        copy.wait()
    values = cache_values[...].reshape(total, kv_local * HD)
    mixed = jnp.dot(low, values, preferred_element_type=F32)
    mixed = mixed.reshape(len(pairs), rows, kv_local * HD)
    own_low = own.astype(BF).astype(F32)
    attended = []
    for i, (g, n) in enumerate(pairs):
        block = slice(g * HD, (g + 1) * HD)
        value = mixed[i][:, block] + own_low[i] * new_value[:, block].astype(F32)
        attended.append((value / denominator[i]).astype(BF))
    attended = jnp.concatenate(attended, 1)
    experts = coefficient_out.shape[1] // 2
    weight = route_weights[...]
    share = weight / jnp.sum(weight, 1, keepdims=True)
    lane = lax.broadcasted_iota(jnp.int32, (rows, experts), 1)
    coefficient = jnp.zeros((rows, experts), F32)
    for k in range(weight.shape[1]):
        coefficient += jnp.where(lane == expert_ids[:, k : k + 1], share[:, k : k + 1], F32(0.0))
    high = coefficient.astype(BF)
    rest = (coefficient - high.astype(F32)).astype(BF)
    coefficient_out[...] = jnp.concatenate([high, rest], 1)
    for copy in copies[8:]:
        copy.wait()
    first = (lax.axis_index("side") == 0) & (lax.axis_index("head") == 0)
    projected = jnp.where(first, hidden[...].astype(F32), F32(0.0))
    for copy, (g, c) in zip(weight_copies, pieces):
        copy.wait()
        low = g * width + c
        projected += jnp.dot(
            attended[:, low : low + step], out_weight[g, c : c + step], preferred_element_type=F32
        )
    partial_out[...] = projected.astype(BF)


def add_kernel(mine, other, out):
    out[...] = (mine[...].astype(F32) + other[...].astype(F32)).astype(BF)


def take_kernel(stream, out):
    width = out.shape[1]
    me = lax.axis_index("head")
    taken = stream[:, :width]
    for h in range(1, stream.shape[1] // width):
        taken = jnp.where(me == h, stream[:, h * width : (h + 1) * width], taken)
    out[...] = taken


def expert_kernel(*refs, width, pieces):
    gathered = in_order(refs[:pieces])
    expert_body(gathered, *refs[pieces:], width, pieces > 1)


def expert_body(gathered, norm_gain, gate_weight, up_weight, down_weight, *rest):
    *outs, inner, width, split = rest
    count, depth, hidden_units = gate_weight.shape
    experts = (gathered.shape[1] - depth) // 2
    rows = gathered.shape[0]
    stream = gathered[:, :depth].astype(F32)
    norm = lax.rsqrt(jnp.mean(stream * stream, -1, keepdims=True) + 1e-06)
    normed = (stream * norm * norm_gain[...]).astype(BF)
    coefficient = gathered[:, depth : depth + experts].astype(F32) + gathered[
        :, depth + experts :
    ].astype(F32)
    lane = lax.broadcasted_iota(jnp.int32, (rows, experts), 1)
    me = lax.axis_index("ep")
    first = (me * lax.axis_size("side") + lax.axis_index("side")) * count
    for e in range(count):
        gate = jnp.dot(normed, gate_weight[e], preferred_element_type=F32)
        upper = jnp.dot(normed, up_weight[e], preferred_element_type=F32)
        share = jnp.sum(jnp.where(lane == first + e, coefficient, F32(0.0)), 1, keepdims=True)
        value = gate / (1.0 + jnp.exp(-gate)) * upper * share
        inner[:, e * hidden_units : (e + 1) * hidden_units] = value.astype(BF)
    result = jnp.dot(
        inner[...],
        down_weight[...].reshape(count * hidden_units, depth),
        preferred_element_type=F32,
    ).astype(BF)
    if split:
        pair = rows // 2
        block = pair // 2
        close = jnp.concatenate([result[block:pair], result[:block]], 0)
        odd = lax.axis_index("side") == 1
        outs[0][...] = jnp.where(odd, close, result[pair:])
        outs[1][...] = jnp.where(odd, result[pair:], close)
        return
    out = outs[0]
    blocks, block_rows, _ = out.shape
    heads = depth // width
    for j in range(blocks // heads):
        target = me ^ j
        for h in range(heads):
            out[target * heads + h] = result[
                j * block_rows : (j + 1) * block_rows, h * width : (h + 1) * width
            ]


def run_experts(gathered, gain, gate_weight, up_weight, down_weight, head_count, ep_count):
    local_count, depth, hidden_units = gate_weight.shape
    rows = gathered[0].shape[0] if len(gathered) > 1 else gathered[0].shape[0] // ep_count
    width = depth // head_count
    if len(gathered) > 1:
        out_shape = [jax.ShapeDtypeStruct((ep_count * rows // 2, depth), BF)] * 2
    else:
        out_shape = [jax.ShapeDtypeStruct((ep_count * head_count, rows, width), BF)]
    weight_bytes = 2 * (gate_weight.size + up_weight.size + down_weight.size)
    return pl.pallas_call(
        functools.partial(expert_kernel, width=width, pieces=len(gathered)),
        out_shape=out_shape,
        in_specs=[VMEM] * (4 + len(gathered)),
        out_specs=[VMEM] * len(out_shape),
        scratch_shapes=[
            pltpu.VMEM((ep_count * rows, local_count * hidden_units), BF),
        ],
        compiler_params=pltpu.CompilerParams(vmem_limit_bytes=8 << 20),
        cost_estimate=pl.CostEstimate(
            flops=ep_count * rows * weight_bytes, bytes_accessed=weight_bytes, transcendentals=0
        ),
        name="experts",
    )(
        *[in_vmem(piece) for piece in gathered],
        in_vmem(gain),
        in_vmem(gate_weight),
        in_vmem(up_weight),
        in_vmem(down_weight),
    )


def on_device(
    hidden,
    query,
    new_key,
    new_value,
    cache_keys,
    cache_values,
    lengths,
    out_weight,
    norm_gain,
    expert_ids,
    route_weights,
    gate_weight,
    up_weight,
    down_weight,
):
    ep_count = lax.axis_size("ep")
    side_count = lax.axis_size("side")
    head_count = lax.axis_size("head")
    rows, depth = hidden.shape
    local_count, _, hidden_units = gate_weight.shape
    experts = local_count * ep_count * side_count
    width = depth // head_count
    top = expert_ids.shape[1]
    gain = norm_gain.reshape(1, depth)
    pieces = out_weight.shape[0] * (out_weight.shape[1] // math.gcd(out_weight.shape[1], 2 * HD))
    partial_value, coefficient, gain_near = pl.pallas_call(
        attend_kernel,
        out_shape=(
            pltpu.VMEM((rows, depth), BF),
            pltpu.VMEM((rows, 2 * experts), BF),
            pltpu.VMEM(gain.shape, F32),
        ),
        in_specs=[HBM] * 11,
        out_specs=(VMEM,) * 3,
        scratch_shapes=[
            pltpu.SMEM(lengths.shape, jnp.int32),
            pltpu.VMEM(query.shape, BF),
            pltpu.VMEM(new_key.shape, BF),
            pltpu.VMEM(new_value.shape, BF),
            pltpu.VMEM(cache_keys.shape, BF),
            pltpu.VMEM(cache_values.shape, BF),
            pltpu.VMEM((rows, top), jnp.int32),
            pltpu.VMEM((rows, top), F32),
            pltpu.VMEM(hidden.shape, BF),
            pltpu.VMEM(out_weight.shape, BF),
            pltpu.SemaphoreType.DMA((10,)),
            pltpu.SemaphoreType.DMA((pieces,)),
        ],
        compiler_params=pltpu.CompilerParams(vmem_limit_bytes=16 << 20),
        cost_estimate=pl.CostEstimate(
            flops=10**12, bytes_accessed=200 * 10**6, transcendentals=0
        ),
        name="attend",
    )(
        in_hbm(lengths),
        in_hbm(query),
        in_hbm(new_key),
        in_hbm(new_value),
        in_hbm(cache_keys),
        in_hbm(cache_values),
        in_hbm(expert_ids),
        in_hbm(route_weights),
        in_hbm(hidden),
        in_hbm(gain),
        in_hbm(out_weight),
    )
    for k in partners(side_count):
        other = swap(partial_value, "side", k)
        partial_value = pl.pallas_call(
            add_kernel,
            out_shape=pltpu.VMEM((rows, depth), BF),
            in_specs=[VMEM] * 2,
            out_specs=VMEM,
            compiler_params=pltpu.CompilerParams(vmem_limit_bytes=4 << 20),
            name="side_sum",
        )(in_vmem(partial_value), in_vmem(other))
    stream = sum_heads(partial_value)
    after_attention = pl.pallas_call(
        take_kernel,
        out_shape=jax.ShapeDtypeStruct((rows, width), F32),
        in_specs=[VMEM],
        out_specs=VMEM,
        compiler_params=pltpu.CompilerParams(vmem_limit_bytes=4 << 20),
        cost_estimate=pl.CostEstimate(flops=10**4, bytes_accessed=10**5, transcendentals=0),
        name="take",
    )(in_vmem(stream))
    packed = jnp.concatenate([stream.astype(BF), coefficient], 1)
    gathered = gather_rows(packed)
    result = run_experts(
        gathered, gain_near, gate_weight, up_weight, down_weight, head_count, ep_count
    )
    if len(result) > 1:
        local_sum = return_rows(*result)
    else:
        arrived = lax.all_to_all(result[0], ("ep", "head"), 0, 0, tiled=True)
        local_sum = jnp.sum(arrived.astype(F32), 0).astype(BF)
    expert_sum = sum_over(local_sum, "side").astype(BF)
    return (after_attention, expert_sum)


def solution(mesh):
    placed = (
        P(("groups", "ep"), None),
        P(("groups", "ep"), "head", "side"),
        P(("groups", "ep"), "head"),
        P(("groups", "ep"), "head"),
        P(("groups", "ep"), None, "head"),
        P(("groups", "ep"), None, "head"),
        P(("groups", "ep")),
        P("head", "side", None),
        P(),
        P(("groups", "ep"), None),
        P(("groups", "ep"), None),
        P(("ep", "side"), None, "head"),
        P(("ep", "side"), None, "head"),
        P(("ep", "side"), "head", None),
    )
    return jax.shard_map(
        on_device,
        mesh=mesh,
        in_specs=placed,
        out_specs=(P(("groups", "ep"), "head"), P(("groups", "ep"), "head")),
        check_vma=False,
    )
```
